512 devices in a mesh: ctx: 32 (over y, x, core), exp: 16 (over z).
Axes of the slice: x: 4, y: 4, z: 16, core: 2. Of those that a mesh axis runs over, the one named last changes fastest.
Arguments:
- queries: bfloat16 [8192, 4096], P('ctx', 'exp'), may hold values from -6 to 6
- key_rows: bfloat16 [8192, 4096], P('ctx', 'exp'), may hold values from -6 to 6
- value_rows: bfloat16 [8192, 4096], P('ctx', 'exp'), may hold values from -6 to 6
- decay_rate: float32 [32], P('exp'), may hold values from 4.8828124e-06 to 0.06
- out_weight: bfloat16 [4096, 3072], P('exp', 'ctx'), may hold values from -0.09375 to 0.09375
- residual: bfloat16 [8192, 3072], P(('ctx', 'exp')), may hold values from -6 to 6
- moe_gain: float32 [3072], replicated, may hold values from 0.1 to 1.9
- expert_ids: int32 [8192, 2], P(('ctx', 'exp')), may hold values from 0 to 15, all different within a row; in each aligned block of 16 rows (0 to 15, 16 to 31, ...) at most 3 rows name the same one
- gate_weight: bfloat16 [16, 4608, 3072], P('exp', 'ctx'), may hold values from -0.109375 to 0.109375
- up_weight: bfloat16 [16, 4608, 3072], P('exp', 'ctx'), may hold values from -0.109375 to 0.109375
Outputs:
- mixed: bfloat16 [8192, 3072], P(('ctx', 'exp'))
- expert_hidden: bfloat16 [16, 4608, 1536], P('exp', 'ctx')
The draws below stay inside these ranges and needn't reach their ends.
Inputs may be any that keep to these rules, and one draw needn't show every extreme that they name: `expert_ids`: in each aligned block of 16 tokens (the rows of one device) no expert is named by more than 3 of the block's routes; some block names some expert exactly 3 times; a token's two ids differ.
All inputs are finite; a program needn't handle non-finite values.
Results may differ from the reference program's by a relative error of at most 0.0079.
Values may be sent and summed in bfloat16 or wider, within the bound.
A program may use at most 64 MiB of HBM per device.

```python
import math
import jax
import jax.numpy as jnp
import numpy as np
from jax import lax

D = 3072
HEAD_DIM = 128
HEADS = 32
HID = 4608
SPAN = 256
SEQ = 8192
TOK_DEV = 16
EXPERTS = 16
CAP = 3
SLOTS = 1536


def levels(rng, extent, shards, smallest, top_value):
    factor_of, own = 1.0, jax.random.fold_in(rng, 6)
    for dim, shards_of in shards:
        steps = jnp.exp(jax.random.uniform(jax.random.fold_in(own, dim), (shards_of,), jnp.float32, smallest / len(shards), top_value / len(shards)))
        factor_of = factor_of * jnp.repeat(steps, extent[dim] // shards_of).reshape([-1 if axis == dim else 1 for axis in range(len(extent))])
    return factor_of


def routed_block(own_key, own, number, rows, amount, top, bound, skew):
    ranking = jax.random.permutation(own_key, amount)
    heavy_load, ordinary = load_shares(amount, rows * top, bound, skew, True), load_shares(amount, rows * top, bound, skew, False)
    places = jnp.arange(amount)

    def named(sizes, offset_by):
        used = int((sizes > 0).sum())
        fixed = max(1, used // 4)
        passed = fixed + (places - fixed + offset_by * (used - fixed)) % max(1, amount - fixed)
        return jnp.zeros((amount,), jnp.int32).at[ranking[jnp.where(places < fixed, places, passed)]].set(jnp.asarray(sizes, jnp.int32))

    sizes = jnp.where(number % 4 == 0, named(heavy_load, number // 4), named(ordinary, number - number // 4 - 1))
    mixed = jax.random.permutation(jax.random.fold_in(own, 3), amount)
    source_of, sink = mixed[0:amount // 2 * 2:2], mixed[1:amount // 2 * 2:2]
    margin = jnp.minimum(sizes[source_of] - 1, bound - sizes[sink]) // 2
    margin = jnp.where((source_of == ranking[0]) | (sink == ranking[0]) | (sizes[sink] == 0), 0, jnp.maximum(margin, 0))
    passed = jax.random.randint(jax.random.fold_in(own, 4), (amount // 2,), 0, 1 << 20) % (margin + 1)
    sizes = sizes.at[source_of].add(-passed).at[sink].add(passed)
    members = jnp.searchsorted(jnp.cumsum(sizes), jnp.arange(rows * top), side="right").astype(jnp.int32)
    table = members.reshape(top, rows).T
    table = table[jax.random.permutation(jax.random.fold_in(own, 1), rows)]
    offset_by = jax.random.randint(jax.random.fold_in(own, 2), (rows, 1), 0, top)
    return jnp.take_along_axis(table, (jnp.arange(top)[None, :] + offset_by) % top, axis=1)


def load_shares(number_of, total, bound, skew, full):
    loads = [(1 << 20) // math.isqrt(rank ** skew) + 1 for rank in range(1, number_of + 1)]
    largest = bound if full else min(bound, max(-(-total // number_of), total * loads[0] // sum(loads)))
    least = 1 if total - largest >= number_of - 1 else 0
    holding, surplus = [largest] + [least] * (number_of - 1), total - largest - least * (number_of - 1)
    while surplus > 0:
        candidates = [i for i in range(1, number_of) if holding[i] < largest] or [i for i in range(1, number_of) if holding[i] < bound]
        pool, remaining = sum([loads[i] for i in candidates]), surplus
        for i in candidates:
            addition = min(bound - holding[i], max(1, remaining * loads[i] // pool), surplus)
            holding[i] = holding[i] + addition
            surplus = surplus - addition
    return np.array(holding)


def gaussian(rng, shape, spread, reach, split=(), kind=jnp.bfloat16):
    array = jax.random.normal(rng, shape, jnp.float32) * spread
    if len(split) > 0:
        array = levels(rng, shape, split, -0.22, 0.18) * array
    return jnp.clip(array, min=-reach, max=reach).astype(kind)


def setup_inputs(seed: int = 0) -> dict:
    splits = jax.random.split(jax.random.key(seed), 11)
    queries = gaussian(splits[0], (SEQ, HEADS * HEAD_DIM), 1.0, 6.0, ((0, 32), (1, 16)))
    key_rows = gaussian(splits[1], (SEQ, HEADS * HEAD_DIM), 1.0, 6.0, ((0, 32), (1, 16)))
    value_rows = gaussian(splits[2], (SEQ, HEADS * HEAD_DIM), 1.0, 6.0, ((0, 32), (1, 16)))
    decay_rate = jnp.clip(jnp.exp(math.log(0.06) - 9.416378 * jax.random.uniform(splits[3], (HEADS,), jnp.float32) ** levels(splits[3], (HEADS,), ((0, 16),), -0.2, 0.2)), 4.882812390860636e-06, 0.06)
    out_weight = gaussian(splits[4], (HEADS * HEAD_DIM, D), (HEADS * HEAD_DIM) ** -0.5, 0.09375, ((0, 16), (1, 32)))
    residual = gaussian(splits[5], (SEQ, D), 1.0, 6.0, ((0, 512),))
    moe_gain = jnp.clip(1.0 + 0.18 * jax.random.normal(splits[6], (D,), jnp.float32), 0.1, 1.9)
    expert_ids_keys = jax.random.split(jax.random.fold_in(splits[7], 1), SEQ // TOK_DEV)
    expert_ids_turns = jax.random.permutation(jax.random.fold_in(splits[7], 3), SEQ // TOK_DEV)
    expert_ids = jax.vmap(lambda own, number: routed_block(jax.random.fold_in(splits[7], 2), own, number, TOK_DEV, EXPERTS, 2, CAP, 2))(expert_ids_keys, expert_ids_turns).reshape((SEQ, 2))
    gate_weight = gaussian(splits[8], (EXPERTS, HID, D), D ** -0.5, 0.109375, ((0, 16), (1, 32)))
    up_weight = gaussian(splits[9], (EXPERTS, HID, D), D ** -0.5, 0.109375, ((0, 16), (1, 32)))
    return dict(queries=queries, key_rows=key_rows, value_rows=value_rows, decay_rate=decay_rate, out_weight=out_weight, residual=residual, moe_gain=moe_gain, expert_ids=expert_ids, gate_weight=gate_weight, up_weight=up_weight)


def route_slots(id_rows):
    count = id_rows.shape[1]
    same = id_rows[:, :, None] == id_rows[:, None, :]
    before = lax.broadcasted_iota(jnp.int32, (count, count), 1) < lax.broadcasted_iota(jnp.int32, (count, count), 0)
    return lax.optimization_barrier(jnp.sum((same & before[None]).astype(jnp.int32), axis=2)).astype(jnp.int32)

def select_matrix(id_rows, slot_rows, owners, capacity):
    routes = id_rows.shape[1]
    places = jnp.arange(capacity, dtype=jnp.int32)
    hits = (id_rows[:, None, None, :] == owners[None, :, None, None]) & (slot_rows[:, None, None, :] == places[None, None, :, None])
    to_token = (jnp.arange(routes, dtype=jnp.int32)[:, None] // 2 == jnp.arange(routes // 2, dtype=jnp.int32)[None, :]).astype(jnp.float32)
    return jnp.einsum('bepr,rt->bept', hits.astype(jnp.float32), to_token)

def reference(queries, key_rows, value_rows, decay_rate, out_weight, residual, moe_gain, expert_ids, gate_weight, up_weight):
    highest = lax.Precision.HIGHEST
    blocks = SEQ // SPAN
    query_blk = queries.reshape(blocks, SPAN, HEADS, HEAD_DIM)
    key_blk = key_rows.reshape(blocks, SPAN, HEADS, HEAD_DIM)
    value_blk = value_rows.reshape(blocks, SPAN, HEADS, HEAD_DIM)
    position = jnp.arange(SPAN, dtype=jnp.float32)
    offset = position[:, None] - position[None, :]
    masked = jnp.where((offset >= 0)[None], jnp.exp(-decay_rate[:, None, None] * jnp.maximum(offset, 0.0)[None]), 0.0)
    inner = jnp.exp(-decay_rate[None, :] * position[:, None])
    tail = jnp.exp(-decay_rate[None, :] * (SPAN - position[:, None]))
    whole = jnp.exp(-decay_rate * SPAN)

    def advance(state, pieces):
        query_f = pieces[0].astype(jnp.float32)
        key_f = pieces[1].astype(jnp.float32)
        value_f = pieces[2].astype(jnp.float32)
        scores = jnp.einsum('ihd,jhd->hij', query_f, key_f, precision=highest)
        weighted = (scores * masked).astype(jnp.bfloat16)
        local_part = jnp.einsum('hij,jhd->ihd', weighted.astype(jnp.float32), value_f, precision=highest)
        carried = jnp.einsum('ihd,hde->ihe', query_f, state, precision=highest) * inner[:, :, None]
        fresh = jnp.einsum('jhd,jhe->hde', key_f * tail[:, :, None], value_f, precision=highest)
        return (whole[:, None, None] * state + fresh, local_part + carried)
    start_state = jnp.zeros((HEADS, HEAD_DIM, HEAD_DIM), jnp.float32)
    unused, attended = lax.scan(advance, start_state, (query_blk, key_blk, value_blk))
    scale_rows = lax.rsqrt(lax.optimization_barrier(jnp.mean(attended * attended, axis=-1, keepdims=True)) + 1e-05)
    head_out = (attended * scale_rows).astype(jnp.bfloat16).reshape(SEQ, HEADS * HEAD_DIM)
    attn = jnp.dot(head_out, out_weight, preferred_element_type=jnp.float32)
    mixed = (residual.astype(jnp.float32) + attn).astype(jnp.bfloat16)
    mixed_f = mixed.astype(jnp.float32)
    normed = (mixed_f * lax.rsqrt(lax.optimization_barrier(jnp.mean(mixed_f * mixed_f, axis=-1, keepdims=True)) + 1e-05) * moe_gain).astype(jnp.bfloat16)
    groups = SEQ // TOK_DEV
    id_rows = expert_ids.reshape(groups, 2 * TOK_DEV).astype(jnp.int32)
    slot_rows = route_slots(id_rows)
    normed_blk = normed.reshape(groups, TOK_DEV, D).astype(jnp.float32)
    contract = (((1,), (1,)), ((), ()))

    def one_expert(items):
        owner, gate_here, up_here = items
        picks = select_matrix(id_rows, slot_rows, jnp.reshape(owner, (1,)), CAP)[:, 0]
        rows = jnp.einsum('bpt,btd->bpd', picks, normed_blk).reshape(SLOTS, D).astype(jnp.bfloat16)
        gated = lax.dot_general(gate_here, rows, contract, preferred_element_type=jnp.float32)
        lifted = lax.dot_general(up_here, rows, contract, preferred_element_type=jnp.float32)
        return (jax.nn.silu(gated) * lifted).astype(jnp.bfloat16)
    expert_hidden = lax.map(one_expert, (jnp.arange(EXPERTS, dtype=jnp.int32), gate_weight, up_weight))
    return (mixed, expert_hidden)
```

```python
import jax
import jax.numpy as jnp
from jax import lax
from jax.experimental import pallas as pl
from jax.experimental.pallas import tpu as pltpu
from jax.sharding import PartitionSpec as P

MESH = pl.DeviceIdType.MESH
F32 = jnp.float32
BF16 = jnp.bfloat16

SIDE = 4
NZ = 16
SPAN = 256
HD = 128
WIDTH = 3072
OWN_COLS = 96
TOK = 16
CAP = 3
ROWS = NZ * CAP
CHUNKS = 3
CW = WIDTH // CHUNKS
KB = CW // 128
PIECES = 6
PW = WIDTH // PIECES
HID_HERE = 144
SLOTS = 1536

A1, A2, B1A, B1B, B2A, B2B, XC, SENT = range(8)


def nt(a, b):
    return lax.dot_general(a, b, (((1,), (1,)), ((), ())), preferred_element_type=F32)


def nn(a, b):
    return jnp.dot(a, b, preferred_element_type=F32)


def iota(shape, dim):
    return lax.broadcasted_iota(jnp.int32, shape, dim)


def one_hot(test):
    return jnp.where(test, 1.0, 0.0).astype(BF16)


def split(x):
    hi = x.astype(BF16)
    return hi, (x - hi.astype(F32)).astype(BF16)


class Gather:
    def __init__(self, whole, half, span, sems, z, core, a, b):
        self.whole, self.half, self.span, self.sems = whole, half, span, sems
        self.z, self.core, self.a, self.b = z, core, a, b

    def at(self, da, db):
        a, b = lax.rem(self.a + (da + SIDE), SIDE), lax.rem(self.b + (db + SIDE), SIDE)
        return self.core + a * (2 + 6 * self.core) + b * (8 - 6 * self.core)

    def send(self, ref, sem, ctx):
        pltpu.make_async_remote_copy(
            src_ref=ref,
            dst_ref=ref,
            send_sem=self.sems.at[SENT],
            recv_sem=self.sems.at[sem],
            device_id=(ctx, self.z),
            device_id_type=MESH,
        ).start()

    def wait(self, sem, blocks):
        ref = self.span(blocks)
        pltpu.make_async_copy(ref, ref, self.sems.at[sem]).wait()

    def across(self, block):
        self.send(self.whole(block), XC, self.at(0, 0) + 1 - 2 * self.core)

    def start(self):
        own = self.whole(self.at(0, 0))
        for d in (1, -1):
            self.send(own, A1, self.at(d, 0))
        for d in (1, -1):
            self.send(own, B1A, self.at(0, d))
        self.across(self.at(0, 0))

    def step1(self):
        self.wait(A1, 2)
        for d in (1, -1):
            block = self.at(-d, 0)
            self.send(self.half(block, (1 - d) // 2), A2, self.at(d, 0))
        for d in (1, -1):
            block = self.at(-d, 0)
            for e in (1, -1):
                self.send(self.whole(block), B1A, self.at(0, e))
            self.across(block)

    def step2(self):
        self.wait(A2, 1)
        block = self.at(2, 0)
        for e in (1, -1):
            self.send(self.whole(block), B1B, self.at(0, e))
        self.across(block)

    def relay(self, da, sem):
        for e in (1, -1):
            block = self.at(da, -e)
            self.send(self.half(block, (1 - e) // 2), sem, self.at(0, e))
            self.across(block)

    def step3(self):
        self.wait(B1A, 6)
        for da in (0, 1, -1):
            self.relay(da, B2A)

    def step4(self):
        self.wait(B1B, 2)
        self.relay(2, B2B)

    def step5(self):
        self.wait(B2A, 3)
        for da in (0, 1, -1):
            self.across(self.at(da, 2))
        self.wait(B2B, 1)
        self.across(self.at(2, 2))

    def arrived(self):
        self.wait(XC, 16)

    def finish(self):
        self.wait(SENT, 31)


def kernel(
    decay, q_hbm, k_hbm, v_hbm, w_hbm, res_hbm, gain_hbm, ids_hbm, gate_hbm, up_hbm,
    mixed_out, hidden_out,
    qb, kb, vb, wb, resb, gainb, idsb, wg, full_w, fr, e1, fx, fy, st, sto, att, ho,
    part, sb, rb, mixf, pick, perm, msg, got, slots, acc,
    load_sem, st_sem, gw_sem, gs_sem, rs_recv, rs_send, c_recv, c_send,
):
    me, z = lax.axis_index("ctx"), lax.axis_index("exp")
    core = lax.rem(me, 2)
    x = lax.rem(me // 2, SIDE)
    y = me // (2 * SIDE)
    a, b = x + core * (y - x), y + core * (x - y)
    partner = me + 1 - 2 * core

    def x_peer(d):
        return me + (lax.rem(x + d, SIDE) - x) * 2

    def y_peer(d):
        return me + (lax.rem(y + d, SIDE) - y) * (2 * SIDE)

    def z_peer(d):
        return lax.rem(z + d, NZ)

    barrier = pltpu.get_barrier_semaphore()

    def greet(ctx, exp):
        pl.semaphore_signal(barrier, inc=1, device_id=(ctx, exp), device_id_type=MESH)

    greet(partner, z)
    for d in range(1, SIDE):
        greet(x_peer(d), z)
        greet(y_peer(d), z)

    @pl.loop(1, NZ)
    def _(d):
        greet(me, z_peer(d))

    loads = [
        pltpu.make_async_copy(src, dst, load_sem.at[i])
        for i, (src, dst) in enumerate(
            (
                (k_hbm, kb), (v_hbm, vb), (w_hbm, wb), (q_hbm, qb), (ids_hbm, idsb),
                (res_hbm, resb), (gain_hbm, gainb),
                (gate_hbm.at[0], full_w.at[pl.ds(0, HID_HERE)]),
                (up_hbm.at[0], full_w.at[pl.ds(HID_HERE, HID_HERE)]),
            )
        )
    ]
    for load in loads:
        load.start()

    eye = one_hot(iota((HD, HD), 0) == iota((HD, HD), 1))

    loads[0].wait()
    loads[1].wait()
    for h in range(2):
        cols = pl.ds(h * HD, HD)
        rate = decay[h]
        tail = jnp.exp(-rate * (SPAN - iota((1, SPAN), 1)).astype(F32))
        hi, lo = split(nt(eye, kb[:, cols]) * tail)
        value = vb[:, cols]
        fr[h] = nn(hi, value) + nn(lo, value)

    loads[2].wait()
    small = one_hot(iota((OWN_COLS, OWN_COLS), 0) == iota((OWN_COLS, OWN_COLS), 1))
    wg[me] = nt(small, wb[...]).astype(BF16)

    weights = Gather(
        lambda n: wg.at[n],
        lambda n, i: wg.at[n, :, pl.ds(i * HD, HD)],
        lambda n: wg.at[pl.ds(0, n)],
        gw_sem, z, core, a, b,
    )

    pl.semaphore_wait(barrier, 1 + 2 * (SIDE - 1) + NZ - 1)

    def state_send(src, dst, i, ctx):
        pltpu.make_async_remote_copy(
            src_ref=src,
            dst_ref=dst,
            send_sem=st_sem.at[4 + i],
            recv_sem=st_sem.at[i],
            device_id=(ctx, z),
            device_id_type=MESH,
        ).start()

    def wait_for(ref, sem):
        pltpu.make_async_copy(ref, ref, sem).wait()

    state_send(fr.at[1 - core], e1, 0, partner)
    weights.start()

    rate_core = decay[core]

    def power(blocks):
        count = jnp.full((1, HD), SPAN, jnp.int32) * blocks
        return jnp.exp(-rate_core * jnp.maximum(count, 0).astype(F32))

    def gated(test, value):
        return jnp.where(test, value, 0.0)

    def local_part(h):
        cols = pl.ds(h * HD, HD)
        rate = decay[h]
        offset = iota((SPAN, SPAN), 0) - iota((SPAN, SPAN), 1)
        masked = jnp.where(
            offset >= 0, jnp.exp(-rate * jnp.maximum(offset, 0).astype(F32)), 0.0
        )
        weighted = (nt(qb[:, cols], kb[:, cols]) * masked).astype(BF16)
        att[h] = nn(weighted, vb[:, cols])

    wait_for(e1, st_sem.at[0])
    own, other = fr[core], e1[...]
    first = jnp.where(core == 0, own, other)
    second = jnp.where(core == 0, other, own)
    e1[...] = first
    fx[x] = (power(1) * first + second).astype(BF16)
    for d in range(1, SIDE):
        state_send(fx.at[x], fx.at[x], 1, x_peer(d))

    loads[3].wait()
    local_part(0)
    weights.step1()

    wait_for(fx.at[pl.ds(0, SIDE - 1)], st_sem.at[1])
    before, total = jnp.zeros((HD, HD), F32), jnp.zeros((HD, HD), F32)
    for i in range(SIDE):
        term = fx[i].astype(F32)
        before = before + gated(i < x, power(2 * (x - 1 - i))) * term
        total = total + power(2 * (SIDE - 1 - i)) * term
    fy[y] = total.astype(BF16)
    for d in range(1, SIDE):
        state_send(fy.at[y], fy.at[y], 2, y_peer(d))

    local_part(1)
    weights.step2()
    weights.step3()

    wait_for(fy.at[pl.ds(0, SIDE - 1)], st_sem.at[2])
    above = jnp.zeros((HD, HD), F32)
    for i in range(SIDE):
        above = above + gated(i < y, power(2 * SIDE * (y - 1 - i))) * fy[i].astype(F32)
    state0 = power(2 * x) * above + before
    state1 = power(1) * state0 + e1[...]
    st[core] = jnp.where(core == 0, state0, state1)
    sto[...] = jnp.where(core == 0, state1, state0)
    state_send(sto, st.at[core], 3, partner)
    weights.step4()

    loads[4].wait()
    lane = iota((TOK, HD), 1)
    expert = lax.shift_right_logical(lane * 43, 7)
    ids = idsb[...]
    named = one_hot((ids[:, 0:1] == expert) | (ids[:, 1:2] == expert))
    lower = one_hot(iota((TOK, TOK), 0) > iota((TOK, TOK), 1))
    rank = nn(lower, named)
    place = (lane - CAP * expert).astype(F32)
    chosen = jnp.where(rank == place, named.astype(F32), 0.0).astype(BF16)
    turned = nt(eye, chosen).astype(BF16)
    tall = (ROWS * KB, HD)
    spread = one_hot(lax.shift_right_logical(iota(tall, 0), 3) == iota(tall, 1))
    again = one_hot(jnp.bitwise_and(lane, TOK - 1) == iota((TOK, HD), 0))
    table = nn(nn(spread, turned).astype(BF16), again)
    here = jnp.bitwise_and(iota(tall, 0), KB - 1) == lax.shift_right_logical(iota(tall, 1), 4)
    pick[...] = jnp.where(here, table, 0.0).astype(BF16)
    square = (ROWS * KB, ROWS * KB)
    block = lax.shift_right_logical(iota(square, 0) * 1366, 16)
    perm[...] = one_hot(iota(square, 1) == KB * (iota(square, 0) - ROWS * block) + block)

    wait_for(st.at[0], st_sem.at[3])
    weights.step5()
    for h in range(2):
        cols = pl.ds(h * HD, HD)
        query = qb[:, cols]
        hi, lo = split(st[h])
        inner = jnp.exp(-decay[h] * iota((SPAN, HD), 0).astype(F32))
        attended = att[h] + (nn(query, hi) + nn(query, lo)) * inner
        mean = jnp.mean(attended * attended, axis=-1, keepdims=True)
        ho[:, cols] = (attended * lax.rsqrt(mean + 1e-05)).astype(BF16)

    weights.arrived()

    def sign(n):
        return 1 if n < PIECES // 2 else -1

    def rs_send_to(i, n, d):
        cols = pl.ds(n * PW, PW)
        pltpu.make_async_remote_copy(
            src_ref=sb.at[i, :, cols],
            dst_ref=rb.at[i, :, cols],
            send_sem=rs_send.at[0],
            recv_sem=rs_recv.at[i, n],
            device_id=(me, z_peer(NZ + d)),
            device_id_type=MESH,
        ).start()

    def wait_piece(i, n):
        wait_for(rb.at[i, :, pl.ds(n * PW, PW)], rs_recv.at[i, n])

    SHORT = NZ // 2
    heads = ho[...]
    flat = wg[...].reshape(WIDTH, SPAN)
    for n in range(PIECES):
        cols = pl.ds(n * PW, PW)
        rows = nt(heads, flat[n * PW : (n + 1) * PW])
        part[:, :, cols] = rows.reshape(NZ, TOK, PW)
        sb[0, :, cols] = part[z_peer(8), :, cols].astype(BF16)
        rs_send_to(0, n, sign(n))
        sb[SHORT, :, cols] = part[z_peer(NZ - 7 * sign(n)), :, cols].astype(BF16)
        rs_send_to(SHORT, n, -sign(n))

    def rs_step(i, n, d, target):
        cols = pl.ds(n * PW, PW)
        wait_piece(i - 1, n)
        value = rb[i - 1, :, cols].astype(F32) + part[target, :, cols]
        sb[i, :, cols] = value.astype(BF16)
        rs_send_to(i, n, d)

    @pl.loop(1, 7)
    def _(i):
        for n in range(PIECES):
            s = sign(n)
            rs_step(i, n, s, z_peer(NZ + s * (8 - i)))
            rs_step(SHORT + i, n, -s, z_peer(NZ - s * (7 - i)))

    for n in range(PIECES):
        rs_step(7, n, sign(n), z_peer(NZ + sign(n)))

    loads[5].wait()
    loads[6].wait()
    squares = jnp.zeros((TOK, HD), F32)
    for n in range(PIECES):
        cols = pl.ds(n * PW, PW)
        wait_piece(SHORT + 6, n)
        wait_piece(7, n)
        value = part[z, :, cols] + (rb[7, :, cols].astype(F32) + rb[SHORT + 6, :, cols].astype(F32))
        rounded = (resb[:, cols].astype(F32) + value).astype(BF16)
        mixed_out[:, cols] = rounded
        rounded = rounded.astype(F32)
        mixf[:, cols] = rounded
        power2 = rounded * rounded
        for i in range(PW // HD):
            squares = squares + power2[:, i * HD : (i + 1) * HD]
    scale = lax.rsqrt(jnp.sum(squares, axis=-1, keepdims=True) / WIDTH + 1e-05)

    def c_copy(j, dest):
        pltpu.make_async_remote_copy(
            src_ref=msg.at[j, dest],
            dst_ref=got.at[j, z],
            send_sem=c_send.at[j],
            recv_sem=c_recv.at[j],
            device_id=(me, dest),
            device_id_type=MESH,
        ).start()

    for j in range(CHUNKS):
        cols = pl.ds(j * CW, CW)
        normed = (mixf[:, cols] * scale * gainb[:, cols]).astype(BF16)
        stacked = jnp.concatenate(
            [normed[:, k * HD : (k + 1) * HD] for k in range(KB)], axis=0
        )
        sent = nn(pick[...], stacked).reshape(NZ, CAP * KB, HD)
        msg[j] = sent.astype(BF16)
        c_copy(j, z_peer(8))

        @pl.loop(1, 8)
        def _(i):
            c_copy(j, z_peer(8 - i))
            c_copy(j, z_peer(8 + i))

        got[j, z] = msg[j, z]

    gathers = [
        Gather(
            lambda n, j=j: slots.at[j, n],
            lambda n, i, j=j: slots.at[j, n, :, pl.ds(i * (CW // 2), CW // 2)],
            lambda n, j=j: slots.at[j, pl.ds(0, n)],
            gs_sem.at[j], z, core, a, b,
        )
        for j in range(CHUNKS)
    ]

    def assemble(j):
        wait_for(got.at[j, pl.ds(0, NZ - 1)], c_recv.at[j])
        rows = got[j].astype(F32).reshape(ROWS * KB, HD).astype(BF16)
        ordered = nn(perm[...], rows).astype(BF16)
        for k in range(KB):
            slots[j, me, :, pl.ds(k * HD, HD)] = ordered[k * ROWS : (k + 1) * ROWS]
        gathers[j].start()

    half_slots = SLOTS // 2

    def experts(j):
        gathers[j].arrived()
        left = full_w[:, pl.ds(j * CW, CW)]
        for i in range(2):
            right = slots[j, pl.ds(i * 16, 16)].reshape(half_slots, CW)
            cols = pl.ds(i * half_slots, half_slots)
            product = nt(left, right)
            if j > 0:
                product = product + acc[:, cols]
            if j < CHUNKS - 1:
                acc[:, cols] = product
            else:
                g, v = product[:HID_HERE], product[HID_HERE:]
                hidden_out[:, cols] = (g / (1.0 + jnp.exp(-g)) * v).astype(BF16)

    g0, g1, g2 = gathers
    assemble(0)
    g0.step1()
    assemble(1)
    g0.step2()
    g1.step1()
    g0.step3()
    g0.step4()
    assemble(2)
    g1.step2()
    g2.step1()
    g0.step5()
    g1.step3()
    g1.step4()
    loads[7].wait()
    loads[8].wait()
    experts(0)
    g2.step2()
    g1.step5()
    g2.step3()
    g2.step4()
    experts(1)
    g2.step5()
    experts(2)

    wait_for(e1, st_sem.at[4])
    wait_for(fx.at[pl.ds(0, SIDE - 1)], st_sem.at[5])
    wait_for(fy.at[pl.ds(0, SIDE - 1)], st_sem.at[6])
    wait_for(sto, st_sem.at[7])
    wait_for(sb, rs_send.at[0])
    weights.finish()
    for j in range(CHUNKS):
        wait_for(msg.at[j, pl.ds(0, NZ - 1)], c_send.at[j])
        gathers[j].finish()


def per_device(queries, keys, values, decay, out_w, residual, gain, ids, gate, up):
    hbm = pl.BlockSpec(memory_space=pl.ANY)
    vmem = pltpu.VMEM
    dma = pltpu.SemaphoreType.DMA
    mixed, hidden = pl.pallas_call(
        kernel,
        out_shape=(
            jax.ShapeDtypeStruct((TOK, WIDTH), BF16),
            jax.ShapeDtypeStruct((HID_HERE, SLOTS), BF16),
        ),
        in_specs=[pl.BlockSpec(memory_space=pltpu.SMEM)] + [hbm] * 9,
        out_specs=(pl.BlockSpec(memory_space=vmem), pl.BlockSpec(memory_space=vmem)),
        scratch_shapes=[
            vmem((SPAN, 2 * HD), BF16),
            vmem((SPAN, 2 * HD), BF16),
            vmem((SPAN, 2 * HD), BF16),
            vmem((SPAN, OWN_COLS), BF16),
            vmem((TOK, WIDTH), BF16),
            vmem((1, WIDTH), F32),
            vmem((TOK, 2), jnp.int32),
            vmem((2 * SIDE * SIDE, OWN_COLS, SPAN), BF16),
            vmem((2 * HID_HERE, WIDTH), BF16),
            vmem((2, HD, HD), F32),
            vmem((HD, HD), F32),
            vmem((SIDE, HD, HD), BF16),
            vmem((SIDE, HD, HD), BF16),
            vmem((2, HD, HD), F32),
            vmem((HD, HD), F32),
            vmem((2, SPAN, HD), F32),
            vmem((SPAN, 2 * HD), BF16),
            vmem((NZ, TOK, WIDTH), F32),
            vmem((NZ - 1, TOK, WIDTH), BF16),
            vmem((NZ - 1, TOK, WIDTH), BF16),
            vmem((TOK, WIDTH), F32),
            vmem((ROWS * KB, HD), BF16),
            vmem((ROWS * KB, ROWS * KB), BF16),
            vmem((CHUNKS, NZ, CAP * KB, HD), BF16),
            vmem((CHUNKS, NZ, CAP * KB, HD), BF16),
            vmem((CHUNKS, 2 * SIDE * SIDE, ROWS, CW), BF16),
            vmem((2 * HID_HERE, SLOTS), F32),
            dma((9,)),
            dma((8,)),
            dma((8,)),
            dma((CHUNKS, 8)),
            dma((NZ - 1, PIECES)),
            dma((1,)),
            dma((CHUNKS,)),
            dma((CHUNKS,)),
        ],
        compiler_params=pltpu.CompilerParams(
            collective_id=0, has_side_effects=True, vmem_limit_bytes=60000000
        ),
        name="block",
    )(
        decay, queries, keys, values, out_w, residual, gain.reshape(1, WIDTH), ids, gate, up
    )
    return mixed, hidden[None]


def solution(mesh):
    in_specs = (
        P("ctx", "exp"),
        P("ctx", "exp"),
        P("ctx", "exp"),
        P("exp"),
        P("exp", "ctx"),
        P(("ctx", "exp"), None),
        P(),
        P(("ctx", "exp"), None),
        P("exp", "ctx", None),
        P("exp", "ctx", None),
    )
    out_specs = (P(("ctx", "exp"), None), P("exp", "ctx", None))
    return jax.shard_map(
        per_device, mesh=mesh, in_specs=in_specs, out_specs=out_specs, check_vma=False
    )
```

```python
import jax
import jax.numpy as jnp
from jax import lax
from jax.experimental import pallas as pl
from jax.experimental.pallas import tpu as pltpu
from jax.sharding import PartitionSpec as P

MESH = pl.DeviceIdType.MESH
F32 = jnp.float32
BF16 = jnp.bfloat16

SIDE = 4
NZ = 16
SPAN = 256
HD = 128
WIDTH = 3072
OWN_COLS = 96
TOK = 16
CAP = 3
ROWS = NZ * CAP
CHUNKS = 3
CW = WIDTH // CHUNKS
KB = CW // 128
PIECES = 6
PW = WIDTH // PIECES
HID_HERE = 144
SLOTS = 1536
PART = SLOTS // SIDE

A1, A2, B1A, B1B, B2A, B2B, XC, SENT = range(8)


def nt(a, b):
    return lax.dot_general(a, b, (((1,), (1,)), ((), ())), preferred_element_type=F32)


def nn(a, b):
    return jnp.dot(a, b, preferred_element_type=F32)


def iota(shape, dim):
    return lax.broadcasted_iota(jnp.int32, shape, dim)


def one_hot(test):
    return jnp.where(test, 1.0, 0.0).astype(BF16)


def split(x):
    hi = x.astype(BF16)
    return hi, (x - hi.astype(F32)).astype(BF16)


class Gather:
    def __init__(self, whole, half, span, sems, z, core, a, b):
        self.whole, self.half, self.span, self.sems = whole, half, span, sems
        self.z, self.core, self.a, self.b = z, core, a, b

    def at(self, da, db):
        a, b = lax.rem(self.a + (da + SIDE), SIDE), lax.rem(self.b + (db + SIDE), SIDE)
        return self.core + a * (2 + 6 * self.core) + b * (8 - 6 * self.core)

    def send(self, ref, sem, ctx):
        pltpu.make_async_remote_copy(
            src_ref=ref,
            dst_ref=ref,
            send_sem=self.sems.at[SENT],
            recv_sem=self.sems.at[sem],
            device_id=(ctx, self.z),
            device_id_type=MESH,
        ).start()

    def wait(self, sem, blocks):
        ref = self.span(blocks)
        pltpu.make_async_copy(ref, ref, self.sems.at[sem]).wait()

    def across(self, block):
        self.send(self.whole(block), XC, self.at(0, 0) + 1 - 2 * self.core)

    def start(self):
        own = self.whole(self.at(0, 0))
        for d in (1, -1):
            self.send(own, A1, self.at(d, 0))
        for d in (1, -1):
            self.send(own, B1A, self.at(0, d))
        self.across(self.at(0, 0))

    def step1(self):
        self.wait(A1, 2)
        for d in (1, -1):
            block = self.at(-d, 0)
            self.send(self.half(block, (1 - d) // 2), A2, self.at(d, 0))
        for d in (1, -1):
            block = self.at(-d, 0)
            for e in (1, -1):
                self.send(self.whole(block), B1A, self.at(0, e))
            self.across(block)

    def step2(self):
        self.wait(A2, 1)
        block = self.at(2, 0)
        for e in (1, -1):
            self.send(self.whole(block), B1B, self.at(0, e))
        self.across(block)

    def relay(self, da, sem):
        for e in (1, -1):
            block = self.at(da, -e)
            self.send(self.half(block, (1 - e) // 2), sem, self.at(0, e))
            self.across(block)

    def step3(self):
        self.wait(B1A, 6)
        for da in (0, 1, -1):
            self.relay(da, B2A)

    def step4(self):
        self.wait(B1B, 2)
        self.relay(2, B2B)

    def step5(self):
        self.wait(B2A, 3)
        for da in (0, 1, -1):
            self.across(self.at(da, 2))
        self.wait(B2B, 1)
        self.across(self.at(2, 2))

    def arrived(self):
        self.wait(XC, 16)

    def finish(self):
        self.wait(SENT, 31)


class Slots:
    def __init__(self, blocks, sems, plane, b, a):
        self.blocks, self.sems, self.plane, self.b, self.a = blocks, sems, plane, b, a
        self.core = plane.core

    def send(self, src, dst, sem, ctx):
        pltpu.make_async_remote_copy(
            src_ref=src,
            dst_ref=dst,
            send_sem=self.sems.at[4],
            recv_sem=self.sems.at[sem],
            device_id=(ctx, self.plane.z),
            device_id_type=MESH,
        ).start()

    def wait(self, sem, count):
        ref = self.blocks.at[pl.ds(0, count)]
        pltpu.make_async_copy(ref, ref, self.sems.at[sem]).wait()

    def along(self, core, sem):
        ref = self.blocks.at[2 * self.b + core]
        for e in (1, -1):
            self.send(ref, ref, sem, self.plane.at(0, e))

    def start(self):
        own = self.blocks.at[2 * self.b + self.core]
        partner = self.plane.at(0, 0) + 1 - 2 * self.core
        self.send(own, self.blocks.at[2 * self.a + self.core], 0, partner)
        self.along(self.core, 1)

    def step1(self):
        self.wait(0, 1)
        self.along(1 - self.core, 2)

    def relay(self, core):
        for e in (1, -1):
            chip = lax.rem(self.b + (SIDE - e), SIDE)
            ref = self.blocks.at[2 * chip + core, :, pl.ds((1 - e) // 2 * (CW // 2), CW // 2)]
            self.send(ref, ref, 3, self.plane.at(0, e))

    def step2(self):
        self.wait(1, 2)
        self.relay(self.core)

    def step3(self):
        self.wait(2, 2)
        self.relay(1 - self.core)

    def arrived(self):
        self.wait(3, 2)

    def finish(self):
        self.wait(4, 7)


def kernel(
    decay, q_hbm, k_hbm, v_hbm, w_hbm, res_hbm, gain_hbm, ids_hbm, gate_hbm, up_hbm,
    mixed_out, hidden_out,
    qb, kb, vb, resb, gainb, idsb, wg, full_w, fr, e1, fx, fy, st, sto, att, ho,
    part, sb, rb, mixf, pick, perm, msg, got, slots, acc, ours, hid,
    load_sem, st_sem, gw_sem, gs_sem, bulk_sem, hid_sem, rs_recv, rs_send, c_recv, c_send,
):
    me, z = lax.axis_index("ctx"), lax.axis_index("exp")
    core = lax.rem(me, 2)
    x = lax.rem(me // 2, SIDE)
    y = me // (2 * SIDE)
    a, b = x + core * (y - x), y + core * (x - y)
    partner = me + 1 - 2 * core

    def x_peer(d):
        return me + (lax.rem(x + d, SIDE) - x) * 2

    def y_peer(d):
        return me + (lax.rem(y + d, SIDE) - y) * (2 * SIDE)

    def z_peer(d):
        return lax.rem(z + d, NZ)

    barrier = pltpu.get_barrier_semaphore()

    def greet(ctx, exp):
        pl.semaphore_signal(barrier, inc=1, device_id=(ctx, exp), device_id_type=MESH)

    greet(partner, z)
    for d in range(1, SIDE):
        greet(x_peer(d), z)
        greet(y_peer(d), z)

    greet(me, z_peer(1))
    greet(me, z_peer(NZ - 1))

    loads = [
        pltpu.make_async_copy(src, dst, load_sem.at[i])
        for i, (src, dst) in enumerate(
            (
                (k_hbm, kb), (v_hbm, vb), (w_hbm, wg.at[me]), (q_hbm, qb), (ids_hbm, idsb),
                (res_hbm, resb), (gain_hbm, gainb),
                (gate_hbm.at[0], full_w.at[a, pl.ds(0, HID_HERE)]),
                (up_hbm.at[0], full_w.at[a, pl.ds(HID_HERE, HID_HERE)]),
            )
        )
    ]
    for load in loads:
        load.start()

    eye = one_hot(iota((HD, HD), 0) == iota((HD, HD), 1))

    loads[0].wait()
    loads[1].wait()
    for h in range(2):
        cols = pl.ds(h * HD, HD)
        rate = decay[h]
        tail = jnp.exp(-rate * (SPAN - iota((1, SPAN), 1)).astype(F32))
        hi, lo = split(nt(eye, kb[:, cols]) * tail)
        value = vb[:, cols]
        fr[h] = nn(hi, value) + nn(lo, value)

    weights = Gather(
        lambda n: wg.at[n],
        lambda n, i: wg.at[n, :, pl.ds(i * HD, HD)],
        lambda n: wg.at[pl.ds(0, n)],
        gw_sem, z, core, a, b,
    )

    pl.semaphore_wait(barrier, 1 + 2 * (SIDE - 1) + 2)
    loads[2].wait()

    def state_send(src, dst, i, ctx):
        pltpu.make_async_remote_copy(
            src_ref=src,
            dst_ref=dst,
            send_sem=st_sem.at[4 + i],
            recv_sem=st_sem.at[i],
            device_id=(ctx, z),
            device_id_type=MESH,
        ).start()

    def wait_for(ref, sem):
        pltpu.make_async_copy(ref, ref, sem).wait()

    state_send(fr.at[1 - core], e1, 0, partner)
    weights.start()

    rate_core = decay[core]

    def power(blocks):
        count = jnp.full((1, HD), SPAN, jnp.int32) * blocks
        return jnp.exp(-rate_core * jnp.maximum(count, 0).astype(F32))

    def gated(test, value):
        return jnp.where(test, value, 0.0)

    def local_part(h):
        cols = pl.ds(h * HD, HD)
        rate = decay[h]
        offset = iota((SPAN, SPAN), 0) - iota((SPAN, SPAN), 1)
        masked = jnp.where(
            offset >= 0, jnp.exp(-rate * jnp.maximum(offset, 0).astype(F32)), 0.0
        )
        weighted = (nt(qb[:, cols], kb[:, cols]) * masked).astype(BF16)
        att[h] = nn(weighted, vb[:, cols])

    wait_for(e1, st_sem.at[0])
    own, other = fr[core], e1[...]
    first = jnp.where(core == 0, own, other)
    second = jnp.where(core == 0, other, own)
    e1[...] = first
    fx[x] = (power(1) * first + second).astype(BF16)
    for d in range(1, SIDE):
        state_send(fx.at[x], fx.at[x], 1, x_peer(d))

    loads[3].wait()
    local_part(0)
    weights.step1()

    wait_for(fx.at[pl.ds(0, SIDE - 1)], st_sem.at[1])
    before, total = jnp.zeros((HD, HD), F32), jnp.zeros((HD, HD), F32)
    for i in range(SIDE):
        term = fx[i].astype(F32)
        before = before + gated(i < x, power(2 * (x - 1 - i))) * term
        total = total + power(2 * (SIDE - 1 - i)) * term
    fy[y] = total.astype(BF16)
    for d in range(1, SIDE):
        state_send(fy.at[y], fy.at[y], 2, y_peer(d))

    local_part(1)
    weights.step2()
    weights.step3()

    wait_for(fy.at[pl.ds(0, SIDE - 1)], st_sem.at[2])
    above = jnp.zeros((HD, HD), F32)
    for i in range(SIDE):
        above = above + gated(i < y, power(2 * SIDE * (y - 1 - i))) * fy[i].astype(F32)
    state0 = power(2 * x) * above + before
    state1 = power(1) * state0 + e1[...]
    st[core] = jnp.where(core == 0, state0, state1)
    sto[...] = jnp.where(core == 0, state1, state0)
    state_send(sto, st.at[core], 3, partner)
    weights.step4()

    loads[4].wait()
    line = iota((HD, TOK), 0)
    expert = lax.shift_right_logical(line * 43, 7)
    named = one_hot((idsb[0:1, :] == expert) | (idsb[1:2, :] == expert))
    upper = one_hot(iota((TOK, TOK), 0) < iota((TOK, TOK), 1))
    rank = nn(named, upper)
    place = (line - CAP * expert).astype(F32)
    turned = jnp.where(rank == place, named.astype(F32), 0.0).astype(BF16)
    tall = (ROWS * KB, HD)
    spread = one_hot(lax.shift_right_logical(iota(tall, 0), 3) == iota(tall, 1))
    again = one_hot(jnp.bitwise_and(iota((TOK, HD), 1), TOK - 1) == iota((TOK, HD), 0))
    table = nn(nn(spread, turned).astype(BF16), again)
    here = jnp.bitwise_and(iota(tall, 0), KB - 1) == lax.shift_right_logical(iota(tall, 1), 4)
    pick[...] = jnp.where(here, table, 0.0).astype(BF16)
    square = (ROWS * KB, ROWS * KB)
    block = lax.shift_right_logical(iota(square, 0) * 1366, 16)
    perm[...] = one_hot(iota(square, 1) == KB * (iota(square, 0) - ROWS * block) + block)

    wait_for(st.at[0], st_sem.at[3])
    weights.step5()
    for h in range(2):
        cols = pl.ds(h * HD, HD)
        query = qb[:, cols]
        hi, lo = split(st[h])
        inner = jnp.exp(-decay[h] * iota((SPAN, HD), 0).astype(F32))
        attended = att[h] + (nn(query, hi) + nn(query, lo)) * inner
        mean = jnp.mean(attended * attended, axis=-1, keepdims=True)
        ho[:, cols] = (attended * lax.rsqrt(mean + 1e-05)).astype(BF16)

    def bulk_send(ref, sem, da):
        pltpu.make_async_remote_copy(
            src_ref=ref,
            dst_ref=ref,
            send_sem=bulk_sem.at[2],
            recv_sem=bulk_sem.at[sem],
            device_id=(weights.at(da, 0), z),
            device_id_type=MESH,
        ).start()

    loads[7].wait()
    loads[8].wait()
    for d in (1, -1):
        bulk_send(full_w.at[a], 0, d)

    weights.arrived()

    def sign(n):
        return 1 if n < PIECES // 2 else -1

    def rs_send_to(i, n, d):
        cols = pl.ds(n * PW, PW)
        pltpu.make_async_remote_copy(
            src_ref=sb.at[i, :, cols],
            dst_ref=rb.at[i, :, cols],
            send_sem=rs_send.at[0],
            recv_sem=rs_recv.at[i, n],
            device_id=(me, z_peer(NZ + d)),
            device_id_type=MESH,
        ).start()

    def wait_piece(i, n):
        wait_for(rb.at[i, :, pl.ds(n * PW, PW)], rs_recv.at[i, n])

    SHORT = NZ // 2
    heads = ho[...]
    flat = wg[...].reshape(WIDTH, SPAN)
    for n in range(PIECES):
        cols = pl.ds(n * PW, PW)
        rows = nt(heads, flat[n * PW : (n + 1) * PW])
        part[:, :, cols] = rows.reshape(NZ, TOK, PW)
        sb[0, :, cols] = part[z_peer(8), :, cols].astype(BF16)
        rs_send_to(0, n, sign(n))
        sb[SHORT, :, cols] = part[z_peer(NZ - 7 * sign(n)), :, cols].astype(BF16)
        rs_send_to(SHORT, n, -sign(n))

    def rs_step(i, n, d, target):
        cols = pl.ds(n * PW, PW)
        wait_piece(i - 1, n)
        value = rb[i - 1, :, cols].astype(F32) + part[target, :, cols]
        sb[i, :, cols] = value.astype(BF16)
        rs_send_to(i, n, d)

    @pl.loop(1, 7)
    def _(i):
        for n in range(PIECES):
            s = sign(n)
            rs_step(i, n, s, z_peer(NZ + s * (8 - i)))
            rs_step(SHORT + i, n, -s, z_peer(NZ - s * (7 - i)))

    for n in range(PIECES):
        rs_step(7, n, sign(n), z_peer(NZ + sign(n)))

    wait_for(full_w.at[pl.ds(0, 2)], bulk_sem.at[0])
    for d in (1, -1):
        chip = lax.rem(a + (SIDE - d), SIDE)
        half = pl.ds((1 - d) // 2 * (WIDTH // 2), WIDTH // 2)
        bulk_send(full_w.at[chip, :, half], 1, d)

    loads[5].wait()
    loads[6].wait()
    squares = jnp.zeros((TOK, HD), F32)
    for n in range(PIECES):
        cols = pl.ds(n * PW, PW)
        wait_piece(SHORT + 6, n)
        wait_piece(7, n)
        value = part[z, :, cols] + (rb[7, :, cols].astype(F32) + rb[SHORT + 6, :, cols].astype(F32))
        rounded = (resb[:, cols].astype(F32) + value).astype(BF16)
        mixed_out[:, cols] = rounded
        rounded = rounded.astype(F32)
        mixf[:, cols] = rounded
        power2 = rounded * rounded
        for i in range(PW // HD):
            squares = squares + power2[:, i * HD : (i + 1) * HD]
    scale = lax.rsqrt(jnp.sum(squares, axis=-1, keepdims=True) / WIDTH + 1e-05)

    def c_copy(j, dest):
        pltpu.make_async_remote_copy(
            src_ref=msg.at[j, dest],
            dst_ref=got.at[j, z],
            send_sem=c_send.at[j],
            recv_sem=c_recv.at[j],
            device_id=(me, dest),
            device_id_type=MESH,
        ).start()

    for j in range(CHUNKS):
        cols = pl.ds(j * CW, CW)
        normed = (mixf[:, cols] * scale * gainb[:, cols]).astype(BF16)
        stacked = jnp.concatenate(
            [normed[:, k * HD : (k + 1) * HD] for k in range(KB)], axis=0
        )
        sent = nn(pick[...], stacked).reshape(NZ, CAP * KB, HD)
        msg[j] = sent.astype(BF16)
        c_copy(j, z_peer(8))

        @pl.loop(1, 8)
        def _(i):
            c_copy(j, z_peer(8 - i))
            c_copy(j, z_peer(8 + i))

        got[j, z] = msg[j, z]

    gathers = [Slots(slots.at[j], gs_sem.at[j], weights, b, a) for j in range(CHUNKS)]

    def assemble(j):
        wait_for(got.at[j, pl.ds(0, NZ - 1)], c_recv.at[j])
        rows = got[j].astype(F32).reshape(ROWS * KB, HD).astype(BF16)
        ordered = nn(perm[...], rows).astype(BF16)
        for k in range(KB):
            slots[j, 2 * b + core, :, pl.ds(k * HD, HD)] = ordered[k * ROWS : (k + 1) * ROWS]
        gathers[j].start()

    def product(j, i):
        right = slots[j].reshape(PART, CW)
        return nt(full_w[i, :, pl.ds(j * CW, CW)], right)

    def experts(j, parts):
        for i in parts:
            if j == 0:
                acc[i] = product(j, i)
            else:
                acc[i] = acc[i] + product(j, i)

    g0, g1, g2 = gathers
    assemble(0)
    g0.step1()
    g0.step2()
    g0.step3()
    assemble(1)
    g1.step1()
    g1.step2()
    g1.step3()
    g0.arrived()
    wait_for(full_w.at[0], bulk_sem.at[1])
    experts(0, (0, 1))
    assemble(2)
    g2.step1()
    experts(0, (2,))
    g2.step2()
    experts(0, (3,))
    g2.step3()
    g1.arrived()
    experts(1, range(SIDE))
    g2.arrived()
    for d in (2, 1, 3, 0):
        i = lax.rem(a + d, SIDE)
        total = acc[i] + product(CHUNKS - 1, i)
        g, v = total[:HID_HERE], total[HID_HERE:]
        value = (g / (1.0 + jnp.exp(-g)) * v).astype(BF16)
        if d == 0:
            hid[a] = value
        else:
            ours[i] = value
            pltpu.make_async_remote_copy(
                src_ref=ours.at[i],
                dst_ref=hid.at[a],
                send_sem=hid_sem.at[1],
                recv_sem=hid_sem.at[0],
                device_id=(weights.at(d, 0), z),
                device_id_type=MESH,
            ).start()
    wait_for(hid.at[pl.ds(0, SIDE - 1)], hid_sem.at[0])

    @pl.when(core == 1)
    def _():
        for i in range(SIDE):
            hidden_out[:, pl.ds(i * PART, PART)] = hid[i]

    @pl.when(core == 0)
    def _():
        step = 2 * ROWS
        for i in range(SIDE):
            pieces = [hid[k].astype(F32)[:, i * step : (i + 1) * step] for k in range(SIDE)]
            hidden_out[:, pl.ds(i * PART, PART)] = jnp.concatenate(pieces, axis=1).astype(BF16)

    wait_for(e1, st_sem.at[4])
    wait_for(fx.at[pl.ds(0, SIDE - 1)], st_sem.at[5])
    wait_for(fy.at[pl.ds(0, SIDE - 1)], st_sem.at[6])
    wait_for(sto, st_sem.at[7])
    wait_for(sb, rs_send.at[0])
    weights.finish()
    wait_for(full_w.at[pl.ds(0, SIDE - 1)], bulk_sem.at[2])
    wait_for(ours.at[pl.ds(0, SIDE - 1)], hid_sem.at[1])
    for j in range(CHUNKS):
        wait_for(msg.at[j, pl.ds(0, NZ - 1)], c_send.at[j])
        gathers[j].finish()


def per_device(queries, keys, values, decay, out_w, residual, gain, ids, gate, up):
    hbm = pl.BlockSpec(memory_space=pl.ANY)
    vmem = pltpu.VMEM
    dma = pltpu.SemaphoreType.DMA
    mixed, hidden = pl.pallas_call(
        kernel,
        out_shape=(
            jax.ShapeDtypeStruct((TOK, WIDTH), BF16),
            jax.ShapeDtypeStruct((HID_HERE, SLOTS), BF16),
        ),
        in_specs=[pl.BlockSpec(memory_space=pltpu.SMEM)] + [hbm] * 9,
        out_specs=(pl.BlockSpec(memory_space=vmem), pl.BlockSpec(memory_space=vmem)),
        scratch_shapes=[
            vmem((SPAN, 2 * HD), BF16),
            vmem((SPAN, 2 * HD), BF16),
            vmem((SPAN, 2 * HD), BF16),
            vmem((TOK, WIDTH), BF16),
            vmem((1, WIDTH), F32),
            vmem((2, TOK), jnp.int32),
            vmem((2 * SIDE * SIDE, OWN_COLS, SPAN), BF16),
            vmem((SIDE, 2 * HID_HERE, WIDTH), BF16),
            vmem((2, HD, HD), F32),
            vmem((HD, HD), F32),
            vmem((SIDE, HD, HD), BF16),
            vmem((SIDE, HD, HD), BF16),
            vmem((2, HD, HD), F32),
            vmem((HD, HD), F32),
            vmem((2, SPAN, HD), F32),
            vmem((SPAN, 2 * HD), BF16),
            vmem((NZ, TOK, WIDTH), F32),
            vmem((NZ - 1, TOK, WIDTH), BF16),
            vmem((NZ - 1, TOK, WIDTH), BF16),
            vmem((TOK, WIDTH), F32),
            vmem((ROWS * KB, HD), BF16),
            vmem((ROWS * KB, ROWS * KB), BF16),
            vmem((CHUNKS, NZ, CAP * KB, HD), BF16),
            vmem((CHUNKS, NZ, CAP * KB, HD), BF16),
            vmem((CHUNKS, 2 * SIDE, ROWS, CW), BF16),
            vmem((SIDE, 2 * HID_HERE, PART), F32),
            vmem((SIDE, HID_HERE, PART), BF16),
            vmem((SIDE, HID_HERE, PART), BF16),
            dma((9,)),
            dma((8,)),
            dma((8,)),
            dma((CHUNKS, 5)),
            dma((3,)),
            dma((2,)),
            dma((NZ - 1, PIECES)),
            dma((1,)),
            dma((CHUNKS,)),
            dma((CHUNKS,)),
        ],
        compiler_params=pltpu.CompilerParams(
            collective_id=0, has_side_effects=True, vmem_limit_bytes=60000000
        ),
        name="block",
    )(
        decay, queries, keys, values, out_w.T, residual, gain.reshape(1, WIDTH), ids.T, gate, up
    )
    return mixed, hidden[None]


def solution(mesh):
    in_specs = (
        P("ctx", "exp"),
        P("ctx", "exp"),
        P("ctx", "exp"),
        P("exp"),
        P("exp", "ctx"),
        P(("ctx", "exp"), None),
        P(),
        P(("ctx", "exp"), None),
        P("exp", "ctx", None),
        P("exp", "ctx", None),
    )
    out_specs = (P(("ctx", "exp"), None), P("exp", "ctx", None))
    return jax.shard_map(
        per_device, mesh=mesh, in_specs=in_specs, out_specs=out_specs, check_vma=False
    )
```

```python
import jax
import jax.numpy as jnp
from jax import lax
from jax.experimental import pallas as pl
from jax.experimental.pallas import tpu as pltpu
from jax.sharding import PartitionSpec as P

MESH = pl.DeviceIdType.MESH
F32 = jnp.float32
BF16 = jnp.bfloat16

SIDE = 4
NZ = 16
SPAN = 256
HD = 128
WIDTH = 3072
OWN_COLS = 96
TOK = 16
CAP = 3
ROWS = NZ * CAP
CHUNKS = 3
CW = WIDTH // CHUNKS
KB = CW // 128
PIECES = 6
PW = WIDTH // PIECES
HID_HERE = 144
SLOTS = 1536
PART = SLOTS // SIDE

A1, A2, B1A, B1B, B2A, B2B, XC, SENT = range(8)


def nt(a, b):
    return lax.dot_general(a, b, (((1,), (1,)), ((), ())), preferred_element_type=F32)


def nn(a, b):
    return jnp.dot(a, b, preferred_element_type=F32)


def iota(shape, dim):
    return lax.broadcasted_iota(jnp.int32, shape, dim)


def one_hot(test):
    return jnp.where(test, 1.0, 0.0).astype(BF16)


def split(x):
    hi = x.astype(BF16)
    return hi, (x - hi.astype(F32)).astype(BF16)


class Gather:
    def __init__(self, whole, half, span, sems, z, core, a, b):
        self.whole, self.half, self.span, self.sems = whole, half, span, sems
        self.z, self.core, self.a, self.b = z, core, a, b

    def at(self, da, db):
        a, b = lax.rem(self.a + (da + SIDE), SIDE), lax.rem(self.b + (db + SIDE), SIDE)
        return self.core + a * (2 + 6 * self.core) + b * (8 - 6 * self.core)

    def send(self, ref, sem, ctx):
        pltpu.make_async_remote_copy(
            src_ref=ref,
            dst_ref=ref,
            send_sem=self.sems.at[SENT],
            recv_sem=self.sems.at[sem],
            device_id=(ctx, self.z),
            device_id_type=MESH,
        ).start()

    def wait(self, sem, blocks):
        ref = self.span(blocks)
        pltpu.make_async_copy(ref, ref, self.sems.at[sem]).wait()

    def across(self, block):
        self.send(self.whole(block), XC, self.at(0, 0) + 1 - 2 * self.core)

    def start(self):
        own = self.whole(self.at(0, 0))
        for d in (1, -1):
            self.send(own, A1, self.at(d, 0))
        for d in (1, -1):
            self.send(own, B1A, self.at(0, d))
        self.across(self.at(0, 0))

    def step1(self):
        self.wait(A1, 2)
        for d in (1, -1):
            block = self.at(-d, 0)
            self.send(self.half(block, (1 - d) // 2), A2, self.at(d, 0))
        for d in (1, -1):
            block = self.at(-d, 0)
            for e in (1, -1):
                self.send(self.whole(block), B1A, self.at(0, e))
            self.across(block)

    def step2(self):
        self.wait(A2, 1)
        block = self.at(2, 0)
        for e in (1, -1):
            self.send(self.whole(block), B1B, self.at(0, e))
        self.across(block)

    def relay(self, da, sem):
        for e in (1, -1):
            block = self.at(da, -e)
            self.send(self.half(block, (1 - e) // 2), sem, self.at(0, e))
            self.across(block)

    def step3(self):
        self.wait(B1A, 6)
        for da in (0, 1, -1):
            self.relay(da, B2A)

    def step4(self):
        self.wait(B1B, 2)
        self.relay(2, B2B)

    def step5(self):
        self.wait(B2A, 3)
        for da in (0, 1, -1):
            self.across(self.at(da, 2))

    def step6(self):
        self.wait(B2B, 1)
        self.across(self.at(2, 2))

    def arrived(self):
        self.wait(XC, 16)

    def finish(self):
        self.wait(SENT, 31)


class Slots:
    def __init__(self, blocks, sems, plane, b, a):
        self.blocks, self.sems, self.plane, self.b, self.a = blocks, sems, plane, b, a
        self.core = plane.core

    def send(self, src, dst, sem, ctx):
        pltpu.make_async_remote_copy(
            src_ref=src,
            dst_ref=dst,
            send_sem=self.sems.at[4],
            recv_sem=self.sems.at[sem],
            device_id=(ctx, self.plane.z),
            device_id_type=MESH,
        ).start()

    def wait(self, sem, count):
        ref = self.blocks.at[pl.ds(0, count)]
        pltpu.make_async_copy(ref, ref, self.sems.at[sem]).wait()

    def start(self):
        own = self.blocks.at[2 * self.b + self.core]
        there = self.blocks.at[2 * self.a + self.core]
        turn = 1 - 2 * self.core
        for e in (1, -1):
            self.send(own, own, 1, self.plane.at(0, e))
        for e in (1, -1):
            self.send(own, there, 2, self.plane.at(e, 0) + turn)
        self.send(own, there, 0, self.plane.at(0, 0) + turn)

    def relay(self, core):
        for e in (1, -1):
            chip = lax.rem(self.b + (SIDE - e), SIDE)
            ref = self.blocks.at[2 * chip + core, :, pl.ds((1 - e) // 2 * (CW // 2), CW // 2)]
            self.send(ref, ref, 3, self.plane.at(0, e))

    def step2(self):
        self.wait(1, 2)
        self.relay(self.core)

    def step3(self):
        self.wait(2, 2)
        self.relay(1 - self.core)

    def arrived(self):
        self.wait(0, 1)
        self.wait(3, 2)

    def finish(self):
        self.wait(4, 7)


def kernel(
    decay, q_hbm, k_hbm, v_hbm, w_hbm, res_hbm, gain_hbm, ids_hbm, gate_hbm, up_hbm,
    mixed_out, hidden_out,
    qb, kb, vb, resb, gainb, idsb, wg, full_w, fr, e1, fx, fy, st, sto, att, ho,
    part, sb, rb, pick, perm, msg, got, slots, acc, ours, hid, mixf,
    load_sem, st_sem, gw_sem, gs_sem, bulk_sem, hid_sem, rs_recv, rs_send, c_recv, c_send,
):
    me, z = lax.axis_index("ctx"), lax.axis_index("exp")
    core = lax.rem(me, 2)
    x = lax.rem(me // 2, SIDE)
    y = me // (2 * SIDE)
    a, b = x + core * (y - x), y + core * (x - y)
    partner = me + 1 - 2 * core

    def x_peer(d):
        return me + (lax.rem(x + d, SIDE) - x) * 2

    def y_peer(d):
        return me + (lax.rem(y + d, SIDE) - y) * (2 * SIDE)

    def z_peer(d):
        return lax.rem(z + d, NZ)

    barrier = pltpu.get_barrier_semaphore()

    def greet(ctx, exp):
        pl.semaphore_signal(barrier, inc=1, device_id=(ctx, exp), device_id_type=MESH)

    greet(partner, z)
    for d in range(1, SIDE):
        greet(x_peer(d), z)
        greet(y_peer(d), z)

    greet(me, z_peer(1))
    greet(me, z_peer(NZ - 1))

    loads = [
        pltpu.make_async_copy(src, dst, load_sem.at[i])
        for i, (src, dst) in enumerate(
            (
                (k_hbm, kb), (v_hbm, vb), (w_hbm, wg.at[me]), (q_hbm, qb), (ids_hbm, idsb),
                (res_hbm, resb), (gain_hbm, gainb),
                (gate_hbm.at[0], full_w.at[a, pl.ds(0, HID_HERE)]),
                (up_hbm.at[0], full_w.at[a, pl.ds(HID_HERE, HID_HERE)]),
            )
        )
    ]
    for load in loads:
        load.start()

    eye = one_hot(iota((HD, HD), 0) == iota((HD, HD), 1))

    loads[0].wait()
    loads[1].wait()
    for h in range(2):
        cols = pl.ds(h * HD, HD)
        rate = decay[h]
        tail = jnp.exp(-rate * (SPAN - iota((1, SPAN), 1)).astype(F32))
        hi, lo = split(nt(eye, kb[:, cols]) * tail)
        value = vb[:, cols]
        fr[h] = nn(hi, value) + nn(lo, value)

    weights = Gather(
        lambda n: wg.at[n],
        lambda n, i: wg.at[n, :, pl.ds(i * HD, HD)],
        lambda n: wg.at[pl.ds(0, n)],
        gw_sem, z, core, a, b,
    )

    pl.semaphore_wait(barrier, 1 + 2 * (SIDE - 1) + 2)
    loads[2].wait()

    def state_send(src, dst, i, ctx):
        pltpu.make_async_remote_copy(
            src_ref=src,
            dst_ref=dst,
            send_sem=st_sem.at[4 + i],
            recv_sem=st_sem.at[i],
            device_id=(ctx, z),
            device_id_type=MESH,
        ).start()

    def wait_for(ref, sem):
        pltpu.make_async_copy(ref, ref, sem).wait()

    state_send(fr.at[1 - core], e1, 0, partner)
    weights.start()

    rate_core = decay[core]

    def power(blocks):
        count = jnp.full((1, HD), SPAN, jnp.int32) * blocks
        return jnp.exp(-rate_core * jnp.maximum(count, 0).astype(F32))

    def gated(test, value):
        return jnp.where(test, value, 0.0)

    def local_part(h):
        cols = pl.ds(h * HD, HD)
        rate = decay[h]
        offset = iota((SPAN, SPAN), 0) - iota((SPAN, SPAN), 1)
        masked = jnp.where(
            offset >= 0, jnp.exp(-rate * jnp.maximum(offset, 0).astype(F32)), 0.0
        )
        weighted = (nt(qb[:, cols], kb[:, cols]) * masked).astype(BF16)
        att[h] = nn(weighted, vb[:, cols])

    wait_for(e1, st_sem.at[0])
    own, other = fr[core], e1[...]
    first = jnp.where(core == 0, own, other)
    second = jnp.where(core == 0, other, own)
    e1[...] = first
    fx[x] = (power(1) * first + second).astype(BF16)
    for d in range(1, SIDE):
        state_send(fx.at[x], fx.at[x], 1, x_peer(d))

    loads[3].wait()
    local_part(0)
    weights.step1()

    wait_for(fx.at[pl.ds(0, SIDE - 1)], st_sem.at[1])
    before, total = jnp.zeros((HD, HD), F32), jnp.zeros((HD, HD), F32)
    for i in range(SIDE):
        term = fx[i].astype(F32)
        before = before + gated(i < x, power(2 * (x - 1 - i))) * term
        total = total + power(2 * (SIDE - 1 - i)) * term
    fy[y] = total.astype(BF16)
    for d in range(1, SIDE):
        state_send(fy.at[y], fy.at[y], 2, y_peer(d))

    local_part(1)
    weights.step2()
    weights.step3()
    weights.step4()
    weights.step5()

    wait_for(fy.at[pl.ds(0, SIDE - 1)], st_sem.at[2])
    above = jnp.zeros((HD, HD), F32)
    for i in range(SIDE):
        above = above + gated(i < y, power(2 * SIDE * (y - 1 - i))) * fy[i].astype(F32)
    state0 = power(2 * x) * above + before
    state1 = power(1) * state0 + e1[...]
    st[core] = jnp.where(core == 0, state0, state1)
    sto[...] = jnp.where(core == 0, state1, state0)
    state_send(sto, st.at[core], 3, partner)
    weights.step6()

    loads[4].wait()
    line = iota((HD, TOK), 0)
    expert = lax.shift_right_logical(line * 43, 7)
    named = one_hot((idsb[0:1, :] == expert) | (idsb[1:2, :] == expert))
    upper = one_hot(iota((TOK, TOK), 0) < iota((TOK, TOK), 1))
    rank = nn(named, upper)
    place = (line - CAP * expert).astype(F32)
    turned = jnp.where(rank == place, named.astype(F32), 0.0).astype(BF16)
    tall = (ROWS * KB, HD)
    spread = one_hot(lax.shift_right_logical(iota(tall, 0), 3) == iota(tall, 1))
    again = one_hot(jnp.bitwise_and(iota((TOK, HD), 1), TOK - 1) == iota((TOK, HD), 0))
    table = nn(nn(spread, turned).astype(BF16), again)
    here = jnp.bitwise_and(iota(tall, 0), KB - 1) == lax.shift_right_logical(iota(tall, 1), 4)
    pick[...] = jnp.where(here, table, 0.0).astype(BF16)
    square = (ROWS * KB, ROWS * KB)
    block = lax.shift_right_logical(iota(square, 0) * 1366, 16)
    perm[...] = one_hot(iota(square, 1) == KB * (iota(square, 0) - ROWS * block) + block)

    wait_for(st.at[0], st_sem.at[3])
    for h in range(2):
        cols = pl.ds(h * HD, HD)
        query = qb[:, cols]
        hi, lo = split(st[h])
        inner = jnp.exp(-decay[h] * iota((SPAN, HD), 0).astype(F32))
        attended = att[h] + (nn(query, hi) + nn(query, lo)) * inner
        mean = jnp.mean(attended * attended, axis=-1, keepdims=True)
        ho[:, cols] = (attended * lax.rsqrt(mean + 1e-05)).astype(BF16)

    def bulk_send(ref, sem, da):
        pltpu.make_async_remote_copy(
            src_ref=ref,
            dst_ref=ref,
            send_sem=bulk_sem.at[2],
            recv_sem=bulk_sem.at[sem],
            device_id=(weights.at(da, 0), z),
            device_id_type=MESH,
        ).start()

    loads[7].wait()
    loads[8].wait()
    for d in (1, -1):
        bulk_send(full_w.at[a], 0, d)

    weights.arrived()

    def sign(n):
        return 1 - 2 * (n % 2)

    def rs_send_to(i, n, d):
        cols = pl.ds(n * PW, PW)
        pltpu.make_async_remote_copy(
            src_ref=sb.at[i, :, cols],
            dst_ref=rb.at[i, :, cols],
            send_sem=rs_send.at[0],
            recv_sem=rs_recv.at[i, n],
            device_id=(me, z_peer(NZ + d)),
            device_id_type=MESH,
        ).start()

    def wait_piece(i, n):
        wait_for(rb.at[i, :, pl.ds(n * PW, PW)], rs_recv.at[i, n])

    SHORT = NZ // 2

    def rs_first(n):
        cols = pl.ds(n * PW, PW)
        columns = wg[...].reshape(WIDTH, SPAN)[n * PW : (n + 1) * PW]
        part[:, :, cols] = nt(ho[...], columns).reshape(NZ, TOK, PW)
        sb[0, :, cols] = part[z_peer(8), :, cols].astype(BF16)
        rs_send_to(0, n, sign(n))
        sb[SHORT, :, cols] = part[z_peer(NZ - 7 * sign(n)), :, cols].astype(BF16)
        rs_send_to(SHORT, n, -sign(n))

    def rs_step(i, n, d, target):
        cols = pl.ds(n * PW, PW)
        wait_piece(i - 1, n)
        value = rb[i - 1, :, cols].astype(F32) + part[target, :, cols]
        sb[i, :, cols] = value.astype(BF16)
        rs_send_to(i, n, d)

    def rs_last(n):
        cols = pl.ds(n * PW, PW)
        wait_piece(SHORT + 6, n)
        wait_piece(7, n)
        value = part[z, :, cols] + (rb[7, :, cols].astype(F32) + rb[SHORT + 6, :, cols].astype(F32))
        rounded = (resb[:, cols].astype(F32) + value).astype(BF16)
        mixed_out[:, cols] = rounded
        rounded = rounded.astype(F32)
        mixf[:, cols] = rounded
        squared = rounded * rounded
        return sum(squared[:, i * HD : (i + 1) * HD] for i in range(PW // HD))

    def c_copy(src, dst, sems, dest):
        pltpu.make_async_remote_copy(
            src_ref=src,
            dst_ref=dst,
            send_sem=sems[0],
            recv_sem=sems[1],
            device_id=(me, dest),
            device_id_type=MESH,
        ).start()

    def to_all(src, dst, sems):
        c_copy(src.at[z_peer(8)], dst.at[z], sems, z_peer(8))

        @pl.loop(1, 8)
        def _(i):
            c_copy(src.at[z_peer(8 - i)], dst.at[z], sems, z_peer(8 - i))
            c_copy(src.at[z_peer(8 + i)], dst.at[z], sems, z_peer(8 + i))

        dst[z] = src[z]

    def dispatch(j, scale):
        cols = pl.ds(j * CW, CW)
        normed = (mixf[:, cols] * scale * gainb[:, cols]).astype(BF16)
        stacked = jnp.concatenate(
            [normed[:, k * HD : (k + 1) * HD] for k in range(KB)], axis=0
        )
        sent = nn(pick[...], stacked).reshape(NZ, CAP * KB, HD)
        msg[j] = sent.astype(BF16)
        to_all(msg.at[j], got.at[j], (c_send.at[j], c_recv.at[j]))

    loads[5].wait()
    loads[6].wait()
    squares = jnp.zeros((TOK, HD), F32)
    for i in range(9):
        if i == 8:
            wait_for(full_w.at[pl.ds(0, 2)], bulk_sem.at[0])
            for d in (1, -1):
                chip = lax.rem(a + (SIDE - d), SIDE)
                half = pl.ds((1 - d) // 2 * (WIDTH // 2), WIDTH // 2)
                bulk_send(full_w.at[chip, :, half], 1, d)
        for n in range(PIECES):
            s = sign(n)
            if i == 0:
                rs_first(n)
            if 1 <= i <= 7:
                rs_step(i, n, s, z_peer(NZ + s * (8 - i)))
            if 1 <= i <= 6:
                rs_step(SHORT + i, n, -s, z_peer(NZ - s * (7 - i)))
            if i == 8:
                squares = squares + rs_last(n)
    scale = lax.rsqrt(jnp.sum(squares, axis=-1, keepdims=True) / WIDTH + 1e-05)
    for j in range(CHUNKS):
        dispatch(j, scale)

    gathers = [Slots(slots.at[j], gs_sem.at[j], weights, b, a) for j in range(CHUNKS)]

    def assemble(j):
        wait_for(got.at[j, pl.ds(0, NZ - 1)], c_recv.at[j])
        rows = got[j].astype(F32).reshape(ROWS * KB, HD).astype(BF16)
        ordered = nn(perm[...], rows).astype(BF16)
        for k in range(KB):
            slots[j, 2 * b + core, :, pl.ds(k * HD, HD)] = ordered[k * ROWS : (k + 1) * ROWS]
        gathers[j].start()

    def product(j, i):
        return nt(full_w[i, :, pl.ds(j * CW, CW)], slots[j].reshape(PART, CW))

    def experts(j):
        for i in range(SIDE):
            if j == 0:
                acc[i] = product(j, i)
            else:
                acc[i] = acc[i] + product(j, i)

    for j in range(CHUNKS):
        assemble(j)
    for g in gathers:
        g.step2()
        g.step3()
    wait_for(full_w.at[0], bulk_sem.at[1])
    for j in range(CHUNKS):
        gathers[j].arrived()
        if j < CHUNKS - 1:
            experts(j)
    for d in (2, 1, 3, 0):
        i = lax.rem(a + d, SIDE)
        total = acc[i] + product(CHUNKS - 1, i)
        g, v = total[:HID_HERE], total[HID_HERE:]
        value = (g / (1.0 + jnp.exp(-g)) * v).astype(BF16)
        if d == 0:
            hid[a] = value
        else:
            ours[i] = value
            pltpu.make_async_remote_copy(
                src_ref=ours.at[i],
                dst_ref=hid.at[a],
                send_sem=hid_sem.at[1],
                recv_sem=hid_sem.at[0],
                device_id=(weights.at(d, 0), z),
                device_id_type=MESH,
            ).start()
    wait_for(hid.at[pl.ds(0, SIDE - 1)], hid_sem.at[0])

    @pl.when(core == 1)
    def _():
        for i in range(SIDE):
            hidden_out[:, pl.ds(i * PART, PART)] = hid[i]

    @pl.when(core == 0)
    def _():
        step = 2 * ROWS
        for i in range(SIDE):
            pieces = [hid[k].astype(F32)[:, i * step : (i + 1) * step] for k in range(SIDE)]
            hidden_out[:, pl.ds(i * PART, PART)] = jnp.concatenate(pieces, axis=1).astype(BF16)

    wait_for(e1, st_sem.at[4])
    wait_for(fx.at[pl.ds(0, SIDE - 1)], st_sem.at[5])
    wait_for(fy.at[pl.ds(0, SIDE - 1)], st_sem.at[6])
    wait_for(sto, st_sem.at[7])
    wait_for(sb, rs_send.at[0])
    weights.finish()
    wait_for(full_w.at[pl.ds(0, SIDE - 1)], bulk_sem.at[2])
    wait_for(ours.at[pl.ds(0, SIDE - 1)], hid_sem.at[1])
    for j in range(CHUNKS):
        wait_for(msg.at[j, pl.ds(0, NZ - 1)], c_send.at[j])
        gathers[j].finish()


def emit(mixed, hidden, mixed_out, hidden_out, mixed_here, hidden_here, sem):
    pairs = [(mixed, mixed_here, mixed_out)]
    for i in range(3):
        rows = pl.ds(i * 48, 48)
        pairs.append((hidden.at[rows], hidden_here.at[rows], hidden_out.at[rows]))
    into = [pltpu.make_async_copy(p[0], p[1], sem.at[0, i]) for i, p in enumerate(pairs)]
    out = [pltpu.make_async_copy(p[1], p[2], sem.at[1, i]) for i, p in enumerate(pairs)]
    for copy in into:
        copy.start()
    for first, second in zip(into, out):
        first.wait()
        second.start()
    for copy in out:
        copy.wait()


def per_device(queries, keys, values, decay, out_w, residual, gain, ids, gate, up):
    hbm = pl.BlockSpec(memory_space=pl.ANY)
    vmem = pltpu.VMEM
    dma = pltpu.SemaphoreType.DMA
    shapes = (
        jax.ShapeDtypeStruct((TOK, WIDTH), BF16),
        jax.ShapeDtypeStruct((HID_HERE, SLOTS), BF16),
    )
    results = pl.pallas_call(
        kernel,
        out_shape=shapes,
        in_specs=[pl.BlockSpec(memory_space=pltpu.SMEM)] + [hbm] * 9,
        out_specs=(pl.BlockSpec(memory_space=vmem), pl.BlockSpec(memory_space=vmem)),
        scratch_shapes=[
            vmem((SPAN, 2 * HD), BF16),
            vmem((SPAN, 2 * HD), BF16),
            vmem((SPAN, 2 * HD), BF16),
            vmem((TOK, WIDTH), BF16),
            vmem((1, WIDTH), F32),
            vmem((2, TOK), jnp.int32),
            vmem((2 * SIDE * SIDE, OWN_COLS, SPAN), BF16),
            vmem((SIDE, 2 * HID_HERE, WIDTH), BF16),
            vmem((2, HD, HD), F32),
            vmem((HD, HD), F32),
            vmem((SIDE, HD, HD), BF16),
            vmem((SIDE, HD, HD), BF16),
            vmem((2, HD, HD), F32),
            vmem((HD, HD), F32),
            vmem((2, SPAN, HD), F32),
            vmem((SPAN, 2 * HD), BF16),
            vmem((NZ, TOK, WIDTH), F32),
            vmem((NZ - 1, TOK, WIDTH), BF16),
            vmem((NZ - 1, TOK, WIDTH), BF16),
            vmem((ROWS * KB, HD), BF16),
            vmem((ROWS * KB, ROWS * KB), BF16),
            vmem((CHUNKS, NZ, CAP * KB, HD), BF16),
            vmem((CHUNKS, NZ, CAP * KB, HD), BF16),
            vmem((CHUNKS, 2 * SIDE, ROWS, CW), BF16),
            vmem((SIDE, 2 * HID_HERE, PART), F32),
            vmem((SIDE, HID_HERE, PART), BF16),
            vmem((SIDE, HID_HERE, PART), BF16),
            vmem((TOK, WIDTH), F32),
            dma((9,)),
            dma((8,)),
            dma((8,)),
            dma((CHUNKS, 5)),
            dma((3,)),
            dma((2,)),
            dma((NZ - 1, PIECES)),
            dma((1,)),
            dma((CHUNKS,)),
            dma((CHUNKS,)),
        ],
        compiler_params=pltpu.CompilerParams(
            collective_id=0, has_side_effects=True, vmem_limit_bytes=60000000
        ),
        name="block",
    )(
        decay, queries, keys, values, out_w.T, residual, gain.reshape(1, WIDTH), ids.T, gate, up
    )
    mixed, hidden = pl.pallas_call(
        emit,
        out_shape=shapes,
        in_specs=[hbm] * 2,
        out_specs=(hbm, hbm),
        scratch_shapes=[vmem((TOK, WIDTH), BF16), vmem((HID_HERE, SLOTS), BF16), dma((2, 4))],
        compiler_params=pltpu.CompilerParams(vmem_limit_bytes=60000000),
        name="emit",
    )(*results)
    return mixed, hidden[None]


def solution(mesh):
    in_specs = (
        P("ctx", "exp"),
        P("ctx", "exp"),
        P("ctx", "exp"),
        P("exp"),
        P("exp", "ctx"),
        P(("ctx", "exp"), None),
        P(),
        P(("ctx", "exp"), None),
        P("exp", "ctx", None),
        P("exp", "ctx", None),
    )
    out_specs = (P(("ctx", "exp"), None), P("exp", "ctx", None))
    return jax.shard_map(
        per_device, mesh=mesh, in_specs=in_specs, out_specs=out_specs, check_vma=False
    )
```

```python
import jax
import jax.numpy as jnp
from jax import lax
from jax.experimental import pallas as pl
from jax.experimental.pallas import tpu as pltpu
from jax.sharding import PartitionSpec as P

MESH = pl.DeviceIdType.MESH
F32 = jnp.float32
BF16 = jnp.bfloat16

SIDE = 4
NZ = 16
SPAN = 256
HD = 128
WIDTH = 3072
OWN_COLS = 96
TOK = 16
CAP = 3
ROWS = NZ * CAP
CHUNKS = 3
CW = WIDTH // CHUNKS
KB = CW // 128
PIECES = 6
PW = WIDTH // PIECES
HID_HERE = 144
SLOTS = 1536
PART = SLOTS // SIDE

A1, A2, B1A, B1B, B2A, B2B, XC, SENT = range(8)


def nt(a, b):
    return lax.dot_general(a, b, (((1,), (1,)), ((), ())), preferred_element_type=F32)


def nn(a, b):
    return jnp.dot(a, b, preferred_element_type=F32)


def iota(shape, dim):
    return lax.broadcasted_iota(jnp.int32, shape, dim)


def one_hot(test):
    return jnp.where(test, 1.0, 0.0).astype(BF16)


def split(x):
    hi = x.astype(BF16)
    return hi, (x - hi.astype(F32)).astype(BF16)


class Gather:
    def __init__(self, whole, half, span, sems, z, core, a, b):
        self.whole, self.half, self.span, self.sems = whole, half, span, sems
        self.z, self.core, self.a, self.b = z, core, a, b

    def at(self, da, db):
        a, b = lax.rem(self.a + (da + SIDE), SIDE), lax.rem(self.b + (db + SIDE), SIDE)
        return self.core + a * (2 + 6 * self.core) + b * (8 - 6 * self.core)

    def send(self, ref, sem, ctx):
        pltpu.make_async_remote_copy(
            src_ref=ref,
            dst_ref=ref,
            send_sem=self.sems.at[SENT],
            recv_sem=self.sems.at[sem],
            device_id=(ctx, self.z),
            device_id_type=MESH,
        ).start()

    def wait(self, sem, blocks):
        ref = self.span(blocks)
        pltpu.make_async_copy(ref, ref, self.sems.at[sem]).wait()

    def across(self, block):
        self.send(self.whole(block), XC, self.at(0, 0) + 1 - 2 * self.core)

    def start(self):
        own = self.whole(self.at(0, 0))
        for d in (1, -1):
            self.send(own, A1, self.at(d, 0))
        for d in (1, -1):
            self.send(own, B1A, self.at(0, d))
        self.across(self.at(0, 0))

    def step1(self):
        self.wait(A1, 2)
        for d in (1, -1):
            block = self.at(-d, 0)
            self.send(self.half(block, (1 - d) // 2), A2, self.at(d, 0))
        for d in (1, -1):
            block = self.at(-d, 0)
            for e in (1, -1):
                self.send(self.whole(block), B1A, self.at(0, e))
            self.across(block)

    def step2(self):
        self.wait(A2, 1)
        block = self.at(2, 0)
        for e in (1, -1):
            self.send(self.whole(block), B1B, self.at(0, e))
        self.across(block)

    def relay(self, da, sem):
        for e in (1, -1):
            block = self.at(da, -e)
            self.send(self.half(block, (1 - e) // 2), sem, self.at(0, e))
            self.across(block)

    def step3(self):
        self.wait(B1A, 6)
        for da in (0, 1, -1):
            self.relay(da, B2A)

    def step4(self):
        self.wait(B1B, 2)
        self.relay(2, B2B)

    def step5(self):
        self.wait(B2A, 3)
        for da in (0, 1, -1):
            self.across(self.at(da, 2))

    def step6(self):
        self.wait(B2B, 1)
        self.across(self.at(2, 2))

    def arrived(self):
        self.wait(XC, 16)

    def finish(self):
        self.wait(SENT, 31)


class Slots:
    def __init__(self, blocks, sems, plane, b, a):
        self.blocks, self.sems, self.plane, self.b, self.a = blocks, sems, plane, b, a
        self.core = plane.core

    def send(self, src, dst, sem, ctx):
        pltpu.make_async_remote_copy(
            src_ref=src,
            dst_ref=dst,
            send_sem=self.sems.at[4],
            recv_sem=self.sems.at[sem],
            device_id=(ctx, self.plane.z),
            device_id_type=MESH,
        ).start()

    def wait(self, sem, count):
        ref = self.blocks.at[pl.ds(0, count)]
        pltpu.make_async_copy(ref, ref, self.sems.at[sem]).wait()

    def start(self):
        own = self.blocks.at[2 * self.b + self.core]
        there = self.blocks.at[2 * self.a + self.core]
        turn = 1 - 2 * self.core
        for e in (1, -1):
            self.send(own, own, 1, self.plane.at(0, e))
        for e in (1, -1):
            self.send(own, there, 2, self.plane.at(e, 0) + turn)
        self.send(own, there, 0, self.plane.at(0, 0) + turn)

    def relay(self, core):
        for e in (1, -1):
            chip = lax.rem(self.b + (SIDE - e), SIDE)
            ref = self.blocks.at[2 * chip + core, :, pl.ds((1 - e) // 2 * (CW // 2), CW // 2)]
            self.send(ref, ref, 3, self.plane.at(0, e))

    def step2(self):
        self.wait(1, 2)
        self.relay(self.core)

    def step3(self):
        self.wait(2, 2)
        self.relay(1 - self.core)

    def arrived(self):
        self.wait(0, 1)
        self.wait(3, 2)

    def finish(self):
        self.wait(4, 7)


def kernel(
    decay, q_hbm, k_hbm, v_hbm, w_hbm, res_hbm, gain_hbm, ids_hbm, gate_hbm, up_hbm,
    mixed_out, hidden_out,
    qb, kb, vb, resb, gainb, idsb, wg, full_w, fr, e1, fx, fy, st, sto, att, ho,
    part, sb, rb, pick, perm, msg, got, slots, acc, ours, hid, mixf,
    load_sem, st_sem, gw_sem, gs_sem, bulk_sem, hid_sem, rs_recv, rs_send, c_recv, c_send,
):
    me, z = lax.axis_index("ctx"), lax.axis_index("exp")
    core = lax.rem(me, 2)
    x = lax.rem(me // 2, SIDE)
    y = me // (2 * SIDE)
    a, b = x + core * (y - x), y + core * (x - y)
    partner = me + 1 - 2 * core

    def x_peer(d):
        return me + (lax.rem(x + d, SIDE) - x) * 2

    def y_peer(d):
        return me + (lax.rem(y + d, SIDE) - y) * (2 * SIDE)

    def z_peer(d):
        return lax.rem(z + d, NZ)

    barrier = pltpu.get_barrier_semaphore()

    def greet(ctx, exp):
        pl.semaphore_signal(barrier, inc=1, device_id=(ctx, exp), device_id_type=MESH)

    greet(partner, z)
    for d in range(1, SIDE):
        greet(x_peer(d), z)
        greet(y_peer(d), z)

    greet(me, z_peer(1))
    greet(me, z_peer(NZ - 1))

    loads = [
        pltpu.make_async_copy(src, dst, load_sem.at[i])
        for i, (src, dst) in enumerate(
            (
                (k_hbm, kb), (v_hbm, vb), (w_hbm, wg.at[me]), (q_hbm, qb), (ids_hbm, idsb),
                (res_hbm, resb), (gain_hbm, gainb),
                (gate_hbm.at[0], full_w.at[a, pl.ds(0, HID_HERE)]),
                (up_hbm.at[0], full_w.at[a, pl.ds(HID_HERE, HID_HERE)]),
            )
        )
    ]
    for load in loads:
        load.start()

    eye = one_hot(iota((HD, HD), 0) == iota((HD, HD), 1))

    loads[0].wait()
    loads[1].wait()
    for h in range(2):
        cols = pl.ds(h * HD, HD)
        rate = decay[h]
        tail = jnp.exp(-rate * (SPAN - iota((1, SPAN), 1)).astype(F32))
        hi, lo = split(nt(eye, kb[:, cols]) * tail)
        value = vb[:, cols]
        fr[h] = nn(hi, value) + nn(lo, value)

    weights = Gather(
        lambda n: wg.at[n],
        lambda n, i: wg.at[n, :, pl.ds(i * HD, HD)],
        lambda n: wg.at[pl.ds(0, n)],
        gw_sem, z, core, a, b,
    )

    pl.semaphore_wait(barrier, 1 + 2 * (SIDE - 1) + 2)
    loads[2].wait()

    def state_send(src, dst, i, ctx):
        pltpu.make_async_remote_copy(
            src_ref=src,
            dst_ref=dst,
            send_sem=st_sem.at[4 + i],
            recv_sem=st_sem.at[i],
            device_id=(ctx, z),
            device_id_type=MESH,
        ).start()

    def wait_for(ref, sem):
        pltpu.make_async_copy(ref, ref, sem).wait()

    state_send(fr.at[1 - core], e1, 0, partner)
    weights.start()

    rate_core = decay[core]

    def power(blocks):
        count = jnp.full((1, HD), SPAN, jnp.int32) * blocks
        return jnp.exp(-rate_core * jnp.maximum(count, 0).astype(F32))

    def gated(test, value):
        return jnp.where(test, value, 0.0)

    def local_part(h):
        cols = pl.ds(h * HD, HD)
        rate = decay[h]
        offset = iota((SPAN, SPAN), 0) - iota((SPAN, SPAN), 1)
        masked = jnp.where(
            offset >= 0, jnp.exp(-rate * jnp.maximum(offset, 0).astype(F32)), 0.0
        )
        weighted = (nt(qb[:, cols], kb[:, cols]) * masked).astype(BF16)
        att[h] = nn(weighted, vb[:, cols])

    wait_for(e1, st_sem.at[0])
    own, other = fr[core], e1[...]
    first = jnp.where(core == 0, own, other)
    second = jnp.where(core == 0, other, own)
    e1[...] = first
    fx[x] = (power(1) * first + second).astype(BF16)
    for d in range(1, SIDE):
        state_send(fx.at[x], fx.at[x], 1, x_peer(d))

    loads[3].wait()
    local_part(0)
    weights.step1()

    wait_for(fx.at[pl.ds(0, SIDE - 1)], st_sem.at[1])
    before, total = jnp.zeros((HD, HD), F32), jnp.zeros((HD, HD), F32)
    for i in range(SIDE):
        term = fx[i].astype(F32)
        before = before + gated(i < x, power(2 * (x - 1 - i))) * term
        total = total + power(2 * (SIDE - 1 - i)) * term
    fy[y] = total.astype(BF16)
    for d in range(1, SIDE):
        state_send(fy.at[y], fy.at[y], 2, y_peer(d))

    local_part(1)
    weights.step2()
    weights.step3()
    weights.step4()
    weights.step5()

    wait_for(fy.at[pl.ds(0, SIDE - 1)], st_sem.at[2])
    above = jnp.zeros((HD, HD), F32)
    for i in range(SIDE):
        above = above + gated(i < y, power(2 * SIDE * (y - 1 - i))) * fy[i].astype(F32)
    state0 = power(2 * x) * above + before
    state1 = power(1) * state0 + e1[...]
    st[core] = jnp.where(core == 0, state0, state1)
    sto[...] = jnp.where(core == 0, state1, state0)
    state_send(sto, st.at[core], 3, partner)
    weights.step6()

    wait_for(st.at[0], st_sem.at[3])
    for h in range(2):
        cols = pl.ds(h * HD, HD)
        query = qb[:, cols]
        hi, lo = split(st[h])
        inner = jnp.exp(-decay[h] * iota((SPAN, HD), 0).astype(F32))
        attended = att[h] + (nn(query, hi) + nn(query, lo)) * inner
        mean = jnp.mean(attended * attended, axis=-1, keepdims=True)
        ho[:, cols] = (attended * lax.rsqrt(mean + 1e-05)).astype(BF16)

    def bulk_send(ref, sem, da):
        pltpu.make_async_remote_copy(
            src_ref=ref,
            dst_ref=ref,
            send_sem=bulk_sem.at[2],
            recv_sem=bulk_sem.at[sem],
            device_id=(weights.at(da, 0), z),
            device_id_type=MESH,
        ).start()

    loads[7].wait()
    loads[8].wait()
    for d in (1, -1):
        bulk_send(full_w.at[a], 0, d)

    weights.arrived()

    def sign(n):
        return 1 - 2 * (n % 2)

    def rs_send_to(i, n, d):
        cols = pl.ds(n * PW, PW)
        pltpu.make_async_remote_copy(
            src_ref=sb.at[i, :, cols],
            dst_ref=rb.at[i, :, cols],
            send_sem=rs_send.at[0],
            recv_sem=rs_recv.at[i, n],
            device_id=(me, z_peer(NZ + d)),
            device_id_type=MESH,
        ).start()

    def wait_piece(i, n):
        wait_for(rb.at[i, :, pl.ds(n * PW, PW)], rs_recv.at[i, n])

    SHORT = NZ // 2

    def rs_first(n):
        cols = pl.ds(n * PW, PW)
        columns = wg[...].reshape(WIDTH, SPAN)[n * PW : (n + 1) * PW]
        part[:, :, cols] = nt(ho[...], columns).reshape(NZ, TOK, PW)
        sb[0, :, cols] = part[z_peer(8), :, cols].astype(BF16)
        rs_send_to(0, n, sign(n))
        sb[SHORT, :, cols] = part[z_peer(NZ - 7 * sign(n)), :, cols].astype(BF16)
        rs_send_to(SHORT, n, -sign(n))

    def rs_step(i, n, d, target):
        cols = pl.ds(n * PW, PW)
        wait_piece(i - 1, n)
        value = rb[i - 1, :, cols].astype(F32) + part[target, :, cols]
        sb[i, :, cols] = value.astype(BF16)
        rs_send_to(i, n, d)

    def rs_last(n):
        cols = pl.ds(n * PW, PW)
        wait_piece(SHORT + 6, n)
        wait_piece(7, n)
        value = part[z, :, cols] + (rb[7, :, cols].astype(F32) + rb[SHORT + 6, :, cols].astype(F32))
        rounded = (resb[:, cols].astype(F32) + value).astype(BF16)
        mixed_out[:, cols] = rounded
        rounded = rounded.astype(F32)
        mixf[:, cols] = rounded
        squared = rounded * rounded
        return sum(squared[:, i * HD : (i + 1) * HD] for i in range(PW // HD))

    def c_copy(src, dst, sems, dest):
        pltpu.make_async_remote_copy(
            src_ref=src,
            dst_ref=dst,
            send_sem=sems[0],
            recv_sem=sems[1],
            device_id=(me, dest),
            device_id_type=MESH,
        ).start()

    def to_all(src, dst, sems):
        c_copy(src.at[z_peer(8)], dst.at[z], sems, z_peer(8))

        @pl.loop(1, 8)
        def _(i):
            c_copy(src.at[z_peer(8 - i)], dst.at[z], sems, z_peer(8 - i))
            c_copy(src.at[z_peer(8 + i)], dst.at[z], sems, z_peer(8 + i))

        dst[z] = src[z]

    def dispatch(j, scale):
        cols = pl.ds(j * CW, CW)
        normed = (mixf[:, cols] * scale * gainb[:, cols]).astype(BF16)
        stacked = jnp.concatenate(
            [normed[:, k * HD : (k + 1) * HD] for k in range(KB)], axis=0
        )
        sent = nn(pick[...], stacked).reshape(NZ, CAP * KB, HD)
        msg[j] = sent.astype(BF16)
        to_all(msg.at[j], got.at[j], (c_send.at[j], c_recv.at[j]))

    def tables():
        loads[4].wait()
        line = iota((HD, TOK), 0)
        expert = lax.shift_right_logical(line * 43, 7)
        named = one_hot((idsb[0:1, :] == expert) | (idsb[1:2, :] == expert))
        upper = one_hot(iota((TOK, TOK), 0) < iota((TOK, TOK), 1))
        rank = nn(named, upper)
        place = (line - CAP * expert).astype(F32)
        turned = jnp.where(rank == place, named.astype(F32), 0.0).astype(BF16)
        tall = (ROWS * KB, HD)
        spread = one_hot(lax.shift_right_logical(iota(tall, 0), 3) == iota(tall, 1))
        again = one_hot(jnp.bitwise_and(iota((TOK, HD), 1), TOK - 1) == iota((TOK, HD), 0))
        table = nn(nn(spread, turned).astype(BF16), again)
        here = jnp.bitwise_and(iota(tall, 0), KB - 1) == lax.shift_right_logical(iota(tall, 1), 4)
        pick[...] = jnp.where(here, table, 0.0).astype(BF16)
        square = (ROWS * KB, ROWS * KB)
        block = lax.shift_right_logical(iota(square, 0) * 1366, 16)
        perm[...] = one_hot(iota(square, 1) == KB * (iota(square, 0) - ROWS * block) + block)

    loads[5].wait()
    loads[6].wait()
    squares = jnp.zeros((TOK, HD), F32)
    for i in range(9):
        if i == 8:
            wait_for(full_w.at[pl.ds(0, 2)], bulk_sem.at[0])
            for d in (1, -1):
                chip = lax.rem(a + (SIDE - d), SIDE)
                half = pl.ds((1 - d) // 2 * (WIDTH // 2), WIDTH // 2)
                bulk_send(full_w.at[chip, :, half], 1, d)
        for n in range(PIECES):
            s = sign(n)
            if i == 0:
                rs_first(n)
            if 1 <= i <= 7:
                rs_step(i, n, s, z_peer(NZ + s * (8 - i)))
            if 1 <= i <= 6:
                rs_step(SHORT + i, n, -s, z_peer(NZ - s * (7 - i)))
            if i == 8:
                squares = squares + rs_last(n)
        if i == 0:
            tables()
    scale = lax.rsqrt(jnp.sum(squares, axis=-1, keepdims=True) / WIDTH + 1e-05)
    for j in range(CHUNKS):
        dispatch(j, scale)

    gathers = [Slots(slots.at[j], gs_sem.at[j], weights, b, a) for j in range(CHUNKS)]

    def assemble(j):
        wait_for(got.at[j, pl.ds(0, NZ - 1)], c_recv.at[j])
        rows = got[j].astype(F32).reshape(ROWS * KB, HD).astype(BF16)
        ordered = nn(perm[...], rows).astype(BF16)
        for k in range(KB):
            slots[j, 2 * b + core, :, pl.ds(k * HD, HD)] = ordered[k * ROWS : (k + 1) * ROWS]
        gathers[j].start()

    def product(j, i):
        return nt(full_w[i, :, pl.ds(j * CW, CW)], slots[j].reshape(PART, CW))

    def experts(j):
        for i in range(SIDE):
            if j == 0:
                acc[i] = product(j, i)
            else:
                acc[i] = acc[i] + product(j, i)

    for j in range(CHUNKS):
        assemble(j)
    for g in gathers:
        g.step2()
        g.step3()
    wait_for(full_w.at[0], bulk_sem.at[1])
    for j in range(CHUNKS):
        gathers[j].arrived()
        if j < CHUNKS - 1:
            experts(j)
    for d in (2, 1, 3, 0):
        i = lax.rem(a + d, SIDE)
        total = acc[i] + product(CHUNKS - 1, i)
        g, v = total[:HID_HERE], total[HID_HERE:]
        value = (g / (1.0 + jnp.exp(-g)) * v).astype(BF16)
        if d == 0:
            hid[a] = value
        else:
            ours[i] = value
            pltpu.make_async_remote_copy(
                src_ref=ours.at[i],
                dst_ref=hid.at[a],
                send_sem=hid_sem.at[1],
                recv_sem=hid_sem.at[0],
                device_id=(weights.at(d, 0), z),
                device_id_type=MESH,
            ).start()
    wait_for(hid.at[pl.ds(0, SIDE - 1)], hid_sem.at[0])

    @pl.when(core == 1)
    def _():
        for i in range(SIDE):
            hidden_out[:, pl.ds(i * PART, PART)] = hid[i]

    @pl.when(core == 0)
    def _():
        step = 2 * ROWS
        for i in range(SIDE):
            pieces = [hid[k].astype(F32)[:, i * step : (i + 1) * step] for k in range(SIDE)]
            hidden_out[:, pl.ds(i * PART, PART)] = jnp.concatenate(pieces, axis=1).astype(BF16)

    wait_for(e1, st_sem.at[4])
    wait_for(fx.at[pl.ds(0, SIDE - 1)], st_sem.at[5])
    wait_for(fy.at[pl.ds(0, SIDE - 1)], st_sem.at[6])
    wait_for(sto, st_sem.at[7])
    wait_for(sb, rs_send.at[0])
    weights.finish()
    wait_for(full_w.at[pl.ds(0, SIDE - 1)], bulk_sem.at[2])
    wait_for(ours.at[pl.ds(0, SIDE - 1)], hid_sem.at[1])
    for j in range(CHUNKS):
        wait_for(msg.at[j, pl.ds(0, NZ - 1)], c_send.at[j])
        gathers[j].finish()


def emit(mixed, hidden, mixed_out, hidden_out, mixed_here, hidden_here, sem):
    pairs = [(mixed, mixed_here, mixed_out)]
    for i in range(3):
        rows = pl.ds(i * 48, 48)
        pairs.append((hidden.at[rows], hidden_here.at[rows], hidden_out.at[rows]))
    into = [pltpu.make_async_copy(p[0], p[1], sem.at[0, i]) for i, p in enumerate(pairs)]
    out = [pltpu.make_async_copy(p[1], p[2], sem.at[1, i]) for i, p in enumerate(pairs)]
    for copy in into:
        copy.start()
    for first, second in zip(into, out):
        first.wait()
        second.start()
    for copy in out:
        copy.wait()


def per_device(queries, keys, values, decay, out_w, residual, gain, ids, gate, up):
    hbm = pl.BlockSpec(memory_space=pl.ANY)
    vmem = pltpu.VMEM
    dma = pltpu.SemaphoreType.DMA
    shapes = (
        jax.ShapeDtypeStruct((TOK, WIDTH), BF16),
        jax.ShapeDtypeStruct((HID_HERE, SLOTS), BF16),
    )
    results = pl.pallas_call(
        kernel,
        out_shape=shapes,
        in_specs=[pl.BlockSpec(memory_space=pltpu.SMEM)] + [hbm] * 9,
        out_specs=(pl.BlockSpec(memory_space=vmem), pl.BlockSpec(memory_space=vmem)),
        scratch_shapes=[
            vmem((SPAN, 2 * HD), BF16),
            vmem((SPAN, 2 * HD), BF16),
            vmem((SPAN, 2 * HD), BF16),
            vmem((TOK, WIDTH), BF16),
            vmem((1, WIDTH), F32),
            vmem((2, TOK), jnp.int32),
            vmem((2 * SIDE * SIDE, OWN_COLS, SPAN), BF16),
            vmem((SIDE, 2 * HID_HERE, WIDTH), BF16),
            vmem((2, HD, HD), F32),
            vmem((HD, HD), F32),
            vmem((SIDE, HD, HD), BF16),
            vmem((SIDE, HD, HD), BF16),
            vmem((2, HD, HD), F32),
            vmem((HD, HD), F32),
            vmem((2, SPAN, HD), F32),
            vmem((SPAN, 2 * HD), BF16),
            vmem((NZ, TOK, WIDTH), F32),
            vmem((NZ - 1, TOK, WIDTH), BF16),
            vmem((NZ - 1, TOK, WIDTH), BF16),
            vmem((ROWS * KB, HD), BF16),
            vmem((ROWS * KB, ROWS * KB), BF16),
            vmem((CHUNKS, NZ, CAP * KB, HD), BF16),
            vmem((CHUNKS, NZ, CAP * KB, HD), BF16),
            vmem((CHUNKS, 2 * SIDE, ROWS, CW), BF16),
            vmem((SIDE, 2 * HID_HERE, PART), F32),
            vmem((SIDE, HID_HERE, PART), BF16),
            vmem((SIDE, HID_HERE, PART), BF16),
            vmem((TOK, WIDTH), F32),
            dma((9,)),
            dma((8,)),
            dma((8,)),
            dma((CHUNKS, 5)),
            dma((3,)),
            dma((2,)),
            dma((NZ - 1, PIECES)),
            dma((1,)),
            dma((CHUNKS,)),
            dma((CHUNKS,)),
        ],
        compiler_params=pltpu.CompilerParams(
            collective_id=0, has_side_effects=True, vmem_limit_bytes=60000000
        ),
        name="block",
    )(
        decay, queries, keys, values, out_w.T, residual, gain.reshape(1, WIDTH), ids.T, gate, up
    )
    mixed, hidden = pl.pallas_call(
        emit,
        out_shape=shapes,
        in_specs=[hbm] * 2,
        out_specs=(hbm, hbm),
        scratch_shapes=[vmem((TOK, WIDTH), BF16), vmem((HID_HERE, SLOTS), BF16), dma((2, 4))],
        compiler_params=pltpu.CompilerParams(vmem_limit_bytes=60000000),
        name="emit",
    )(*results)
    return mixed, hidden[None]


def solution(mesh):
    in_specs = (
        P("ctx", "exp"),
        P("ctx", "exp"),
        P("ctx", "exp"),
        P("exp"),
        P("exp", "ctx"),
        P(("ctx", "exp"), None),
        P(),
        P(("ctx", "exp"), None),
        P("exp", "ctx", None),
        P("exp", "ctx", None),
    )
    out_specs = (P(("ctx", "exp"), None), P("exp", "ctx", None))
    return jax.shard_map(
        per_device, mesh=mesh, in_specs=in_specs, out_specs=out_specs, check_vma=False
    )
```
